128 devices in a mesh: ctx: 32 (over z, x, core), tp: 4 (over y).
Axes of the slice: x: 4, y: 4, z: 4, core: 2. Of those that a mesh axis runs over, the one named last changes fastest.
Arguments:
- tokens: bfloat16 [4096, 4096], P('ctx', 'tp'), may hold values from -6 to 6
- in_weight: bfloat16 [4096, 3, 4096], P('ctx', None, 'tp'), may hold values from -0.09375 to 0.09375
- conv_taps: float32 [3, 3, 4096], P(None, None, 'tp'), may hold values from -2.5 to 2.5
- decay_rate: float32 [16, 4096], P(None, 'tp'), may hold values from 0 to 0.034, as said below
- residue: float32 [16, 4096], P(None, 'tp'), may hold values from -1 to 1
- skip: float32 [4096], P('tp'), may hold values from -1 to 1
Outputs:
- mixed: bfloat16 [4096, 4096], P('ctx', 'tp')
The draws below stay inside these ranges and needn't reach their ends.
Inputs may be any that keep to these rules, and one draw needn't show every extreme that they name: `decay_rate`: positive decay rates of the poles.
All inputs are finite; a program needn't handle non-finite values.
Results may differ from the reference program's by a relative error of at most 0.0063.
Values may be sent and summed in bfloat16 or wider, within the bound.
A program may use at most 128 MiB of HBM per device.

```python
import math
import jax
import jax.numpy as jnp
from jax import lax

D = 4096
POLES = 16
SEQ = 4096


def modal_parts(key):
    base = jax.random.fold_in(key, 4242)
    key_pick, key_slow, key_fast, key_res = jax.random.split(base, 4)
    share = 5
    picked = jax.random.randint(key_pick, (POLES, D), 0, 10) < share
    slow = jnp.exp(jax.random.uniform(key_slow, (POLES, D), jnp.float32, math.log(0.1), math.log(2.3))) / SEQ
    slow = jnp.minimum(slow, 0.0333)
    fast = jnp.exp(jax.random.uniform(key_fast, (POLES, D), jnp.float32, math.log(0.02), math.log(1.0 / 30.0)))
    rate = jnp.where(picked, slow, fast)
    spread = jnp.clip(jax.random.normal(key_res, (POLES, D), jnp.float32), -3.5, 3.5)
    resid = 0.28 * spread * jnp.sqrt(1.0 - jnp.exp(-2.0 * rate))
    return (rate, resid)


def draw_decay_rate(key, part):
    return modal_parts(key)[0]


def draw_residue(key, part):
    return modal_parts(key)[1]


def steps_of(own_key, extent, shards, least, high):
    def one(axis_at, parts):
        draws = jax.random.uniform(jax.random.fold_in(jax.random.fold_in(own_key, 6), axis_at), (parts,), jnp.float32, least / len(shards), high / len(shards))
        return jnp.repeat(jnp.exp(draws), extent[axis_at] // parts).reshape((-1,) + (1,) * (len(extent) - axis_at - 1))

    level = one(*shards[0])
    for cut in shards[1:]:
        level = level * one(*cut)
    return level


def gaussian(own_key, shape, scale, bound, pieces=(), held_as=jnp.bfloat16):
    result = jax.random.normal(own_key, shape, jnp.float32) * scale
    if len(pieces) > 0:
        result = steps_of(own_key, shape, pieces, -0.22, 0.18) * result
    return jnp.clip(result, min=-bound, max=bound).astype(held_as)


def setup_inputs(seed: int = 0) -> dict:
    arg_keys = jax.random.split(jax.random.key(seed), 7)
    return {
        "tokens": gaussian(arg_keys[0], (SEQ, D), 1.0, 6.0, ((0, 32), (1, 4))),
        "in_weight": gaussian(arg_keys[1], (D, 3, D), D ** -0.5, 0.09375, ((0, 32), (2, 4))),
        "conv_taps": gaussian(arg_keys[2], (3, 3, D), 0.6, 2.5, ((2, 4),), jnp.float32),
        "decay_rate": draw_decay_rate(jax.random.fold_in(arg_keys[6], 71), 0),
        "residue": draw_residue(jax.random.fold_in(arg_keys[6], 71), 0),
        "skip": jnp.clip(jax.random.uniform(arg_keys[5], (D,), jnp.float32, -1.0, 1.0) * steps_of(arg_keys[5], (D,), ((0, 4),), -0.4, 0.0), -1.0, 1.0),
    }


def reference(tokens, in_weight, conv_taps, decay_rate, residue, skip):
    group = 512 if D % 512 == 0 else D

    def one_group(start):
        weight = lax.dynamic_slice_in_dim(in_weight, start, group, 2)
        taps = lax.dynamic_slice_in_dim(conv_taps, start, group, 2)
        rate = lax.dynamic_slice_in_dim(decay_rate, start, group, 1)
        resid = lax.dynamic_slice_in_dim(residue, start, group, 1)
        direct = lax.dynamic_slice_in_dim(skip, start, group, 0)
        streams = []
        for stream in range(3):
            rounded = jnp.dot(tokens, weight[:, stream, :], preferred_element_type=jnp.float32).astype(jnp.bfloat16)
            values = lax.optimization_barrier(rounded).astype(jnp.float32)
            padded = jnp.concatenate([jnp.zeros((2, group), jnp.float32), values], axis=0)
            out = taps[0, stream] * padded[2:] + taps[1, stream] * padded[1:-1] + taps[2, stream] * padded[:-2]
            streams.append(out)
        gated = streams[1] * streams[2]
        decay = jnp.exp(-rate)

        def advance(state, item):
            state = decay * state + item[None, :]
            return state, jnp.sum(resid * state, axis=0)

        _, convolved = lax.scan(advance, jnp.zeros((POLES, group), jnp.float32), gated)
        return (streams[0] * (convolved + direct[None, :] * gated)).astype(jnp.bfloat16)

    starts = jnp.arange(D // group, dtype=jnp.int32) * group
    blocks = lax.map(one_group, starts)
    return jnp.transpose(blocks, (1, 0, 2)).reshape(SEQ, D)
```

```python
import jax
import jax.numpy as jnp
from jax import lax
from jax.experimental import pallas as pl
from jax.experimental.pallas import tpu as pltpu
from jax.sharding import PartitionSpec as P

LANES = 128


def passed_along(array, axis, by):
    peers = lax.axis_size(axis)
    pairs = [(i, i + by) for i in range(peers) if 0 <= i + by < peers]
    return lax.ppermute(array, axis, pairs)


def filtered_at(x_ref, taps_ref, g, t):
    return (
        taps_ref[0, g] * x_ref[g, t + 2]
        + taps_ref[1, g] * x_ref[g, t + 1]
        + taps_ref[2, g] * x_ref[g, t]
    )


def local_end_kernel(x_ref, taps_ref, decay_ref, end_ref):
    rows = x_ref.shape[1] - 2

    def step(t, state):
        gated = filtered_at(x_ref, taps_ref, 1, t) * filtered_at(x_ref, taps_ref, 2, t)
        return decay_ref[...] * state + gated[None]

    end_ref[...] = lax.fori_loop(
        0, rows, step, jnp.zeros(end_ref.shape, jnp.float32), unroll=8
    )


def mixed_kernel(
    x_ref, taps_ref, decay_ref, resid_ref, skip_ref, ends_ref, span_ref, here_ref, out_ref
):
    rows = x_ref.shape[1] - 2
    here = here_ref[0]

    def gather_carry(k, carry):
        later = span_ref[...] * carry + ends_ref[k]
        return jnp.where(k < here, later, carry)

    start = lax.fori_loop(
        0, ends_ref.shape[0], gather_carry, jnp.zeros(decay_ref.shape, jnp.float32)
    )

    def step(t, state):
        query = filtered_at(x_ref, taps_ref, 0, t)
        gated = filtered_at(x_ref, taps_ref, 1, t) * filtered_at(x_ref, taps_ref, 2, t)
        state = decay_ref[...] * state + gated[None]
        convolved = jnp.sum(resid_ref[...] * state, axis=0)
        out_ref[t] = query * (convolved + skip_ref[...] * gated)
        return state

    lax.fori_loop(0, rows, step, start, unroll=8)


def vmem_specs(n):
    return [pl.BlockSpec(memory_space=pltpu.VMEM)] * n


def per_device(tokens, in_weight, conv_taps, decay_rate, residue, skip):
    rows = tokens.shape[0]
    chans = in_weight.shape[2]
    poles = decay_rate.shape[0]
    subl = chans // LANES
    whole = lax.all_gather(tokens, "tp", axis=1, tiled=True)
    piece = lax.all_gather(in_weight, "ctx", axis=0, tiled=True)
    sums = tuple(
        (jnp.dot(whole, piece[:, g, :], preferred_element_type=jnp.float32) for g in range(3))
    )
    projected = jnp.stack([total.astype(jnp.bfloat16) for total in sums], axis=0)
    edge_out = passed_along(projected[:, rows - 2 :, :], "ctx", 1)
    extended = jnp.concatenate([edge_out, projected], axis=1)
    values = lax.optimization_barrier(extended).astype(jnp.float32)
    x = values.reshape(3, rows + 2, subl, LANES)
    taps = conv_taps.reshape(3, 3, subl, LANES)
    decay = jnp.exp(-decay_rate).reshape(poles, subl, LANES)
    span = jnp.exp(-decay_rate * float(rows)).reshape(poles, subl, LANES)
    resid = residue.reshape(poles, subl, LANES)
    direct = skip.reshape(subl, LANES)

    end = pl.pallas_call(
        local_end_kernel,
        out_shape=jax.ShapeDtypeStruct((poles, subl, LANES), jnp.float32),
        in_specs=vmem_specs(3),
        out_specs=pl.BlockSpec(memory_space=pltpu.VMEM),
    )(x, taps, decay)
    ends = lax.all_gather(end, "ctx", axis=0)
    here = lax.axis_index("ctx").astype(jnp.int32).reshape(1)
    out = pl.pallas_call(
        mixed_kernel,
        out_shape=jax.ShapeDtypeStruct((rows, subl, LANES), jnp.float32),
        in_specs=vmem_specs(7) + [pl.BlockSpec(memory_space=pltpu.SMEM)],
        out_specs=pl.BlockSpec(memory_space=pltpu.VMEM),
    )(x, taps, decay, resid, direct, ends, span, here)
    return out.reshape(rows, chans).astype(jnp.bfloat16)


def solution(mesh):
    placed = (
        P("ctx", "tp"),
        P("ctx", None, "tp"),
        P(None, None, "tp"),
        P(None, "tp"),
        P(None, "tp"),
        P("tp"),
    )
    return jax.shard_map(
        per_device, mesh=mesh, in_specs=placed, out_specs=P("ctx", "tp"), check_vma=False
    )
```

```python
import jax
import jax.numpy as jnp
from jax import lax
from jax.experimental import pallas as pl
from jax.experimental.pallas import tpu as pltpu
from jax.sharding import PartitionSpec as P

LANES = 128


def filtered_at(x_ref, taps_ref, g, t):
    return (
        taps_ref[0, g] * x_ref[g, t + 2]
        + taps_ref[1, g] * x_ref[g, t + 1]
        + taps_ref[2, g] * x_ref[g, t]
    )


def local_end_kernel(x_ref, taps_ref, decay_ref, end_ref):
    rows = x_ref.shape[1] - 2

    def step(t, state):
        gated = filtered_at(x_ref, taps_ref, 1, t) * filtered_at(x_ref, taps_ref, 2, t)
        return decay_ref[...] * state + gated[None]

    end_ref[...] = lax.fori_loop(
        0, rows, step, jnp.zeros(end_ref.shape, jnp.float32), unroll=8
    )


def mixed_kernel(x_ref, taps_ref, decay_ref, resid_ref, skip_ref, start_ref, out_ref):
    rows = x_ref.shape[1] - 2

    def step(t, state):
        query = filtered_at(x_ref, taps_ref, 0, t)
        gated = filtered_at(x_ref, taps_ref, 1, t) * filtered_at(x_ref, taps_ref, 2, t)
        state = decay_ref[...] * state + gated[None]
        convolved = jnp.sum(resid_ref[...] * state, axis=0)
        out_ref[t] = query * (convolved + skip_ref[...] * gated)
        return state

    lax.fori_loop(0, rows, step, start_ref[...], unroll=8)


def vmem_specs(n):
    return [pl.BlockSpec(memory_space=pltpu.VMEM)] * n


def shifted(array, axes, by):
    peers = 1
    for axis in axes:
        peers *= lax.axis_size(axis)
    pairs = [(i, i + by) for i in range(peers) if i + by < peers]
    return lax.ppermute(array, axes, pairs)


def swapped(array, axis):
    return lax.ppermute(array, axis, [(0, 1), (1, 0)])


def gathered_tp(tokens):
    peers, here = lax.axis_size("tp"), lax.axis_index("tp")
    blocks = [tokens]
    for by in range(1, peers):
        blocks.append(lax.ppermute(tokens, "tp", [(i, (i + by) % peers) for i in range(peers)]))
    stacked = jnp.stack(blocks, axis=0)
    order = (here - jnp.arange(peers)) % peers
    placed = jnp.take(stacked, jnp.argsort(order), axis=0)
    return jnp.transpose(placed, (1, 0, 2)).reshape(tokens.shape[0], -1)


def per_device(tokens, in_weight, conv_taps, decay_rate, residue, skip):
    ctx = ("cx", "core")
    rows = tokens.shape[0]
    chans = in_weight.shape[2]
    poles = decay_rate.shape[0]
    subl = chans // LANES
    core = lax.axis_index("core")
    piece = lax.all_gather(in_weight, "cx", axis=0, tiled=True)
    whole = gathered_tp(tokens)
    split = whole.reshape(rows, -1, 2, in_weight.shape[0])
    mine = jnp.where(core == 0, split[:, :, 0], split[:, :, 1]).reshape(rows, -1)
    theirs = jnp.where(core == 0, split[:, :, 1], split[:, :, 0]).reshape(rows, -1)
    both = jnp.concatenate([mine, swapped(theirs, "core")], axis=0)
    partial = jnp.stack(
        [jnp.dot(both, piece[:, g, :], preferred_element_type=jnp.float32) for g in range(3)],
        axis=0,
    )
    sums = partial[:, :rows] + swapped(partial[:, rows:], "core")
    projected = sums.astype(jnp.bfloat16)
    edge_out = shifted(projected[:, rows - 2 :, :], ctx, 1)
    extended = jnp.concatenate([edge_out, projected], axis=1)
    values = lax.optimization_barrier(extended).astype(jnp.float32)
    x = values.reshape(3, rows + 2, subl, LANES)
    taps = conv_taps.reshape(3, 3, subl, LANES)
    decay = jnp.exp(-decay_rate).reshape(poles, subl, LANES)
    resid = residue.reshape(poles, subl, LANES)
    direct = skip.reshape(subl, LANES)

    end = pl.pallas_call(
        local_end_kernel,
        out_shape=jax.ShapeDtypeStruct((poles, subl, LANES), jnp.float32),
        in_specs=vmem_specs(3),
        out_specs=pl.BlockSpec(memory_space=pltpu.VMEM),
    )(x, taps, decay)
    start = shifted(end, ctx, 1)
    peers = lax.axis_size("cx") * lax.axis_size("core")
    by = 1
    while by < peers:
        span = jnp.exp(-decay_rate * float(rows * by)).reshape(poles, subl, LANES)
        start = start + span * shifted(start, ctx, by)
        by *= 2
    out = pl.pallas_call(
        mixed_kernel,
        out_shape=jax.ShapeDtypeStruct((rows, subl, LANES), jnp.float32),
        in_specs=vmem_specs(6),
        out_specs=pl.BlockSpec(memory_space=pltpu.VMEM),
    )(x, taps, decay, resid, direct, start)
    return out.reshape(rows, chans).astype(jnp.bfloat16)


def solution(mesh):
    ctx, tp = mesh.shape["ctx"], mesh.shape["tp"]
    split = jax.sharding.Mesh(mesh.devices.reshape(ctx // 2, 2, tp), ("cx", "core", "tp"))
    c = ("cx", "core")
    placed = (
        P(c, "tp"),
        P(c, None, "tp"),
        P(None, None, "tp"),
        P(None, "tp"),
        P(None, "tp"),
        P("tp"),
    )
    return jax.shard_map(
        per_device, mesh=split, in_specs=placed, out_specs=P(c, "tp"), check_vma=False
    )
```

```python
import functools

import jax
import jax.numpy as jnp
from jax import lax
from jax.experimental import pallas as pl
from jax.experimental.pallas import tpu as pltpu
from jax.sharding import PartitionSpec as P

MESH = pl.DeviceIdType.MESH

LANES = 128


def filtered_at(x_ref, taps_ref, g, t):
    return (
        taps_ref[0, g] * x_ref[g, t + 2]
        + taps_ref[1, g] * x_ref[g, t + 1]
        + taps_ref[2, g] * x_ref[g, t]
    )


def local_end_kernel(x_ref, taps_ref, decay_ref, end_ref):
    rows = x_ref.shape[1] - 2

    def step(t, state):
        gated = filtered_at(x_ref, taps_ref, 1, t) * filtered_at(x_ref, taps_ref, 2, t)
        return decay_ref[...] * state + gated[None]

    end_ref[...] = lax.fori_loop(
        0, rows, step, jnp.zeros(end_ref.shape, jnp.float32), unroll=8
    )


def mixed_kernel(x_ref, taps_ref, decay_ref, resid_ref, skip_ref, start_ref, out_ref):
    rows = x_ref.shape[1] - 2

    def step(t, state):
        query = filtered_at(x_ref, taps_ref, 0, t)
        gated = filtered_at(x_ref, taps_ref, 1, t) * filtered_at(x_ref, taps_ref, 2, t)
        state = decay_ref[...] * state + gated[None]
        convolved = jnp.sum(resid_ref[...] * state, axis=0)
        out_ref[t] = query * (convolved + skip_ref[...] * gated)
        return state

    lax.fori_loop(0, rows, step, start_ref[...], unroll=8)


def carry_kernel(peers, end_ref, lift_ref, keep_ref, start_ref, held, slots, send_sem, recv_sem):
    rounds = lift_ref.shape[0]
    me = lax.axis_index("cx") * 2 + lax.axis_index("core")
    tp = lax.axis_index("tp")

    def device(i):
        return (i // 2, i % 2, tp)

    barrier = pltpu.get_barrier_semaphore()
    for r in range(rounds):
        for peer in ((me + 2**r) % peers, (me + peers - 2**r) % peers):
            pl.semaphore_signal(barrier, inc=1, device_id=device(peer), device_id_type=MESH)
    pl.semaphore_wait(barrier, 2 * rounds)

    held[0] = end_ref[...]
    start_ref[...] = jnp.zeros(start_ref.shape, jnp.float32)
    copies = []
    for r in range(rounds):
        copy = pltpu.make_async_remote_copy(
            src_ref=held.at[r],
            dst_ref=slots.at[r],
            send_sem=send_sem.at[r],
            recv_sem=recv_sem.at[r],
            device_id=device((me + 2**r) % peers),
            device_id_type=MESH,
        )
        copy.start()
        copies.append(copy)
        copy.wait_recv()
        got = jnp.where(me >= 2**r, slots[r], 0.0)
        start_ref[...] += lift_ref[r] * got
        if r + 1 < rounds:
            held[r + 1] = held[r] + keep_ref[r] * got
    for copy in copies:
        copy.wait_send()


def vmem_specs(n):
    return [pl.BlockSpec(memory_space=pltpu.VMEM)] * n


def shifted(array, axes, by):
    peers = 1
    for axis in axes:
        peers *= lax.axis_size(axis)
    pairs = [(i, i + by) for i in range(peers) if i + by < peers]
    return lax.ppermute(array, axes, pairs)


def swapped(array, axis):
    return lax.ppermute(array, axis, [(0, 1), (1, 0)])


def gathered_tp(tokens):
    peers, here = lax.axis_size("tp"), lax.axis_index("tp")
    blocks = [tokens]
    for by in range(1, peers):
        blocks.append(lax.ppermute(tokens, "tp", [(i, (i + by) % peers) for i in range(peers)]))
    stacked = jnp.stack(blocks, axis=0)
    order = (here - jnp.arange(peers)) % peers
    placed = jnp.take(stacked, jnp.argsort(order), axis=0)
    return jnp.transpose(placed, (1, 0, 2)).reshape(tokens.shape[0], -1)


def per_device(tokens, in_weight, conv_taps, decay_rate, residue, skip):
    ctx = ("cx", "core")
    rows = tokens.shape[0]
    chans = in_weight.shape[2]
    poles = decay_rate.shape[0]
    subl = chans // LANES
    core = lax.axis_index("core")
    piece = lax.all_gather(in_weight, "cx", axis=0, tiled=True)
    whole = gathered_tp(tokens)
    split = whole.reshape(rows, -1, 2, in_weight.shape[0])
    mine = jnp.where(core == 0, split[:, :, 0], split[:, :, 1]).reshape(rows, -1)
    theirs = jnp.where(core == 0, split[:, :, 1], split[:, :, 0]).reshape(rows, -1)
    both = jnp.concatenate([mine, swapped(theirs, "core")], axis=0)
    partial = jnp.stack(
        [jnp.dot(both, piece[:, g, :], preferred_element_type=jnp.float32) for g in range(3)],
        axis=0,
    )
    sums = partial[:, :rows] + swapped(partial[:, rows:], "core")
    projected = sums.astype(jnp.bfloat16)
    edge_out = shifted(projected[:, rows - 2 :, :], ctx, 1)
    extended = jnp.concatenate([edge_out, projected], axis=1)
    values = lax.optimization_barrier(extended).astype(jnp.float32)
    x = values.reshape(3, rows + 2, subl, LANES)
    taps = conv_taps.reshape(3, 3, subl, LANES)
    decay = jnp.exp(-decay_rate).reshape(poles, subl, LANES)
    resid = residue.reshape(poles, subl, LANES)
    direct = skip.reshape(subl, LANES)

    end = pl.pallas_call(
        local_end_kernel,
        out_shape=jax.ShapeDtypeStruct((poles, subl, LANES), jnp.float32),
        in_specs=vmem_specs(3),
        out_specs=pl.BlockSpec(memory_space=pltpu.VMEM),
    )(x, taps, decay)
    peers = lax.axis_size("cx") * lax.axis_size("core")
    rounds = max(1, (peers - 1).bit_length())
    widths = jnp.asarray([2.0**r for r in range(rounds)], jnp.float32)[:, None, None]
    lift = jnp.exp(-decay_rate[None] * (rows * (widths - 1.0))).reshape(rounds, poles, subl, LANES)
    keep = jnp.exp(-decay_rate[None] * (rows * widths)).reshape(rounds, poles, subl, LANES)
    state_shape = (poles, subl, LANES)
    start = pl.pallas_call(
        functools.partial(carry_kernel, peers),
        out_shape=jax.ShapeDtypeStruct(state_shape, jnp.float32),
        in_specs=vmem_specs(3),
        out_specs=pl.BlockSpec(memory_space=pltpu.VMEM),
        scratch_shapes=[
            pltpu.VMEM((rounds,) + state_shape, jnp.float32),
            pltpu.VMEM((rounds,) + state_shape, jnp.float32),
            pltpu.SemaphoreType.DMA((rounds,)),
            pltpu.SemaphoreType.DMA((rounds,)),
        ],
        compiler_params=pltpu.CompilerParams(collective_id=0, has_side_effects=True),
    )(end, lift, keep)
    out = pl.pallas_call(
        mixed_kernel,
        out_shape=jax.ShapeDtypeStruct((rows, subl, LANES), jnp.float32),
        in_specs=vmem_specs(6),
        out_specs=pl.BlockSpec(memory_space=pltpu.VMEM),
    )(x, taps, decay, resid, direct, start)
    return out.reshape(rows, chans).astype(jnp.bfloat16)


def solution(mesh):
    ctx, tp = mesh.shape["ctx"], mesh.shape["tp"]
    split = jax.sharding.Mesh(mesh.devices.reshape(ctx // 2, 2, tp), ("cx", "core", "tp"))
    c = ("cx", "core")
    placed = (
        P(c, "tp"),
        P(c, None, "tp"),
        P(None, None, "tp"),
        P(None, "tp"),
        P(None, "tp"),
        P("tp"),
    )
    return jax.shard_map(
        per_device, mesh=split, in_specs=placed, out_specs=P(c, "tp"), check_vma=False
    )
```

```python
import functools

import jax
import jax.numpy as jnp
from jax import lax
from jax.experimental import pallas as pl
from jax.experimental.pallas import tpu as pltpu
from jax.sharding import PartitionSpec as P

MESH = pl.DeviceIdType.MESH

LANES = 128


def filtered_at(x_ref, taps_ref, g, t):
    return (
        taps_ref[0, g] * x_ref[g, t + 2]
        + taps_ref[1, g] * x_ref[g, t + 1]
        + taps_ref[2, g] * x_ref[g, t]
    )


def local_end_kernel(x_ref, taps_ref, decay_ref, end_ref):
    rows = x_ref.shape[1] - 2

    def step(t, state):
        gated = filtered_at(x_ref, taps_ref, 1, t) * filtered_at(x_ref, taps_ref, 2, t)
        return decay_ref[...] * state + gated[None]

    end_ref[...] = lax.fori_loop(
        0, rows, step, jnp.zeros(end_ref.shape, jnp.float32), unroll=8
    )


def mixed_kernel(x_ref, taps_ref, decay_ref, resid_ref, skip_ref, start_ref, out_ref):
    rows = x_ref.shape[1] - 2

    def step(t, state):
        query = filtered_at(x_ref, taps_ref, 0, t)
        gated = filtered_at(x_ref, taps_ref, 1, t) * filtered_at(x_ref, taps_ref, 2, t)
        state = decay_ref[...] * state + gated[None]
        convolved = jnp.sum(resid_ref[...] * state, axis=0)
        out_ref[t] = query * (convolved + skip_ref[...] * gated)
        return state

    lax.fori_loop(0, rows, step, start_ref[...], unroll=8)


def carry_kernel(peers, digits, end_ref, lift_ref, keep_ref, start_ref, held, slots, send_sem, recv_sem):
    me = lax.axis_index("cx") * 2 + lax.axis_index("core")
    tp = lax.axis_index("tp")

    def device(i):
        return (i // 2, i % 2, tp)

    steps = []
    width = 1
    for r, digit in enumerate(digits):
        steps.extend((r, d * width) for d in range(1, digit))
        width *= digit

    barrier = pltpu.get_barrier_semaphore()
    for _, by in steps:
        for peer in ((me + by) % peers, (me + peers - by) % peers):
            pl.semaphore_signal(barrier, inc=1, device_id=device(peer), device_id_type=MESH)
    pl.semaphore_wait(barrier, 2 * len(steps))

    held[0] = end_ref[...]
    start_ref[...] = jnp.zeros(start_ref.shape, jnp.float32)
    copies = []
    for r in range(len(digits)):
        mine = [(n, by) for n, (q, by) in enumerate(steps) if q == r]
        for n, by in mine:
            copy = pltpu.make_async_remote_copy(
                src_ref=held.at[r],
                dst_ref=slots.at[n],
                send_sem=send_sem.at[n],
                recv_sem=recv_sem.at[n],
                device_id=device((me + by) % peers),
                device_id_type=MESH,
            )
            copy.start()
            copies.append(copy)
        grown = held[r]
        for n, by in mine:
            copies[n].wait_recv()
            got = jnp.where(me >= by, slots[n], 0.0)
            start_ref[...] += lift_ref[n] * got
            grown = grown + keep_ref[n] * got
        if r + 1 < len(digits):
            held[r + 1] = grown
    for copy in copies:
        copy.wait_send()


def scan_digits(peers):
    digits = []
    while peers > 1:
        digit = 4 if peers % 4 == 0 and peers != 8 else 2
        digits.append(digit)
        peers //= digit
    return digits or [2]


def vmem_specs(n):
    return [pl.BlockSpec(memory_space=pltpu.VMEM)] * n


def shifted(array, axes, by):
    peers = 1
    for axis in axes:
        peers *= lax.axis_size(axis)
    pairs = [(i, i + by) for i in range(peers) if i + by < peers]
    return lax.ppermute(array, axes, pairs)


def swapped(array, axis):
    return lax.ppermute(array, axis, [(0, 1), (1, 0)])


def gathered_tp(tokens):
    peers, here = lax.axis_size("tp"), lax.axis_index("tp")
    blocks = [tokens]
    for by in range(1, peers):
        blocks.append(lax.ppermute(tokens, "tp", [(i, (i + by) % peers) for i in range(peers)]))
    stacked = jnp.stack(blocks, axis=0)
    order = (here - jnp.arange(peers)) % peers
    placed = jnp.take(stacked, jnp.argsort(order), axis=0)
    return jnp.transpose(placed, (1, 0, 2)).reshape(tokens.shape[0], -1)


def per_device(tokens, in_weight, conv_taps, decay_rate, residue, skip):
    ctx = ("cx", "core")
    rows = tokens.shape[0]
    chans = in_weight.shape[2]
    poles = decay_rate.shape[0]
    subl = chans // LANES
    core = lax.axis_index("core")
    piece = lax.all_gather(in_weight, "cx", axis=0, tiled=True)
    whole = gathered_tp(tokens)
    split = whole.reshape(rows, -1, 2, in_weight.shape[0])
    mine = jnp.where(core == 0, split[:, :, 0], split[:, :, 1]).reshape(rows, -1)
    theirs = jnp.where(core == 0, split[:, :, 1], split[:, :, 0]).reshape(rows, -1)
    both = jnp.concatenate([mine, swapped(theirs, "core")], axis=0)
    partial = jnp.stack(
        [jnp.dot(both, piece[:, g, :], preferred_element_type=jnp.float32) for g in range(3)],
        axis=0,
    )
    sums = partial[:, :rows] + swapped(partial[:, rows:], "core")
    projected = sums.astype(jnp.bfloat16)
    edge_out = shifted(projected[:, rows - 2 :, :], ctx, 1)
    extended = jnp.concatenate([edge_out, projected], axis=1)
    values = lax.optimization_barrier(extended).astype(jnp.float32)
    x = values.reshape(3, rows + 2, subl, LANES)
    taps = conv_taps.reshape(3, 3, subl, LANES)
    decay = jnp.exp(-decay_rate).reshape(poles, subl, LANES)
    resid = residue.reshape(poles, subl, LANES)
    direct = skip.reshape(subl, LANES)

    end = pl.pallas_call(
        local_end_kernel,
        out_shape=jax.ShapeDtypeStruct((poles, subl, LANES), jnp.float32),
        in_specs=vmem_specs(3),
        out_specs=pl.BlockSpec(memory_space=pltpu.VMEM),
    )(x, taps, decay)
    peers = lax.axis_size("cx") * lax.axis_size("core")
    digits = scan_digits(peers)
    strides, width = [], 1
    for digit in digits:
        strides.extend(d * width for d in range(1, digit))
        width *= digit
    copies = len(strides)
    widths = jnp.asarray(strides, jnp.float32)[:, None, None]
    lift = jnp.exp(-decay_rate[None] * (rows * (widths - 1.0))).reshape(copies, poles, subl, LANES)
    keep = jnp.exp(-decay_rate[None] * (rows * widths)).reshape(copies, poles, subl, LANES)
    state_shape = (poles, subl, LANES)
    start = pl.pallas_call(
        functools.partial(carry_kernel, peers, digits),
        out_shape=jax.ShapeDtypeStruct(state_shape, jnp.float32),
        in_specs=vmem_specs(3),
        out_specs=pl.BlockSpec(memory_space=pltpu.VMEM),
        scratch_shapes=[
            pltpu.VMEM((len(digits),) + state_shape, jnp.float32),
            pltpu.VMEM((copies,) + state_shape, jnp.float32),
            pltpu.SemaphoreType.DMA((copies,)),
            pltpu.SemaphoreType.DMA((copies,)),
        ],
        compiler_params=pltpu.CompilerParams(collective_id=0, has_side_effects=True),
    )(end, lift, keep)
    out = pl.pallas_call(
        mixed_kernel,
        out_shape=jax.ShapeDtypeStruct((rows, subl, LANES), jnp.float32),
        in_specs=vmem_specs(6),
        out_specs=pl.BlockSpec(memory_space=pltpu.VMEM),
    )(x, taps, decay, resid, direct, start)
    return out.reshape(rows, chans).astype(jnp.bfloat16)


def solution(mesh):
    ctx, tp = mesh.shape["ctx"], mesh.shape["tp"]
    split = jax.sharding.Mesh(mesh.devices.reshape(ctx // 2, 2, tp), ("cx", "core", "tp"))
    c = ("cx", "core")
    placed = (
        P(c, "tp"),
        P(c, None, "tp"),
        P(None, None, "tp"),
        P(None, "tp"),
        P(None, "tp"),
        P("tp"),
    )
    return jax.shard_map(
        per_device, mesh=split, in_specs=placed, out_specs=P(c, "tp"), check_vma=False
    )
```

```python
import functools

import jax
import jax.numpy as jnp
from jax import lax
from jax.experimental import pallas as pl
from jax.experimental.pallas import tpu as pltpu
from jax.sharding import PartitionSpec as P

MESH = pl.DeviceIdType.MESH

LANES = 128


def filtered_at(x_ref, taps_ref, g, t):
    return (
        taps_ref[0, g] * x_ref[g, t + 2]
        + taps_ref[1, g] * x_ref[g, t + 1]
        + taps_ref[2, g] * x_ref[g, t]
    )


def local_end_kernel(x_ref, taps_ref, decay_ref, end_ref):
    rows = x_ref.shape[1] - 2

    def step(t, state):
        gated = filtered_at(x_ref, taps_ref, 1, t) * filtered_at(x_ref, taps_ref, 2, t)
        return decay_ref[...] * state + gated[None]

    end_ref[...] = lax.fori_loop(
        0, rows, step, jnp.zeros(end_ref.shape, jnp.float32), unroll=8
    )


def mixed_kernel(x_ref, taps_ref, decay_ref, resid_ref, skip_ref, start_ref, out_ref):
    rows = x_ref.shape[1] - 2

    def step(t, state):
        query = filtered_at(x_ref, taps_ref, 0, t)
        gated = filtered_at(x_ref, taps_ref, 1, t) * filtered_at(x_ref, taps_ref, 2, t)
        state = decay_ref[...] * state + gated[None]
        convolved = jnp.sum(resid_ref[...] * state, axis=0)
        out_ref[t] = query * (convolved + skip_ref[...] * gated)
        return state

    lax.fori_loop(0, rows, step, start_ref[...], unroll=8)


def carry_kernel(peers, digits, end_ref, lift_ref, keep_ref, start_ref, held, slots, send_sem, recv_sem):
    me = lax.axis_index("cx") * 2 + lax.axis_index("core")
    tp = lax.axis_index("tp")

    def device(i):
        return (i // 2, i % 2, tp)

    steps = []
    width = 1
    for r, digit in enumerate(digits):
        steps.extend((r, d * width) for d in range(1, digit))
        width *= digit

    barrier = pltpu.get_barrier_semaphore()
    for _, by in steps:
        for peer in ((me + by) % peers, (me + peers - by) % peers):
            pl.semaphore_signal(barrier, inc=1, device_id=device(peer), device_id_type=MESH)
    pl.semaphore_wait(barrier, 2 * len(steps))

    held[0] = end_ref[...]
    start_ref[...] = jnp.zeros(start_ref.shape, jnp.float32)
    copies = []
    for r in range(len(digits)):
        mine = [(n, by) for n, (q, by) in enumerate(steps) if q == r]
        for n, by in mine:
            copy = pltpu.make_async_remote_copy(
                src_ref=held.at[r],
                dst_ref=slots.at[n],
                send_sem=send_sem.at[n],
                recv_sem=recv_sem.at[n],
                device_id=device((me + by) % peers),
                device_id_type=MESH,
            )
            copy.start()
            copies.append(copy)
        grown = held[r]
        for n, by in mine:
            copies[n].wait_recv()
            got = jnp.where(me >= by, slots[n], 0.0)
            start_ref[...] += lift_ref[n] * got
            grown = grown + keep_ref[n] * got
        if r + 1 < len(digits):
            held[r + 1] = grown
    for copy in copies:
        copy.wait_send()


def scan_digits(peers):
    digits = []
    while peers > 1:
        digit = 4 if peers % 4 == 0 and peers != 8 else 2
        digits.append(digit)
        peers //= digit
    return digits or [2]


def vmem_specs(n):
    return [pl.BlockSpec(memory_space=pltpu.VMEM)] * n


def shifted(array, axes, by):
    peers = 1
    for axis in axes:
        peers *= lax.axis_size(axis)
    pairs = [(i, i + by) for i in range(peers) if i + by < peers]
    return lax.ppermute(array, axes, pairs)


def swapped(array, axis):
    return lax.ppermute(array, axis, [(0, 1), (1, 0)])


def gathered_tp(tokens):
    peers, here = lax.axis_size("tp"), lax.axis_index("tp")
    blocks = [tokens]
    for by in range(1, peers):
        blocks.append(lax.ppermute(tokens, "tp", [(i, (i + by) % peers) for i in range(peers)]))
    stacked = jnp.stack(blocks, axis=0)
    order = (here - jnp.arange(peers)) % peers
    placed = jnp.take(stacked, jnp.argsort(order), axis=0)
    return jnp.transpose(placed, (1, 0, 2)).reshape(tokens.shape[0], -1)


def block_half(both, piece, conv_taps, decay_rate, residue, skip, rows, tag):
    ctx = ("cx", "core")
    chans = piece.shape[2]
    poles = decay_rate.shape[0]
    subl = chans // LANES
    partial = jnp.stack(
        [jnp.dot(both, piece[:, g, :], preferred_element_type=jnp.float32) for g in range(3)],
        axis=0,
    )
    sums = partial[:, :rows] + swapped(partial[:, rows:], "core")
    projected = sums.astype(jnp.bfloat16)
    edge_out = shifted(projected[:, rows - 2 :, :], ctx, 1)
    extended = jnp.concatenate([edge_out, projected], axis=1)
    values = lax.optimization_barrier(extended).astype(jnp.float32)
    x = values.reshape(3, rows + 2, subl, LANES)
    taps = conv_taps.reshape(3, 3, subl, LANES)
    decay = jnp.exp(-decay_rate).reshape(poles, subl, LANES)
    resid = residue.reshape(poles, subl, LANES)
    direct = skip.reshape(subl, LANES)

    end = pl.pallas_call(
        local_end_kernel,
        out_shape=jax.ShapeDtypeStruct((poles, subl, LANES), jnp.float32),
        in_specs=vmem_specs(3),
        out_specs=pl.BlockSpec(memory_space=pltpu.VMEM),
        cost_estimate=pl.CostEstimate(
            flops=40 * rows * poles * chans, transcendentals=0, bytes_accessed=x.size * 4
        ),
    )(x, taps, decay)
    peers = lax.axis_size("cx") * lax.axis_size("core")
    digits = scan_digits(peers)
    strides, width = [], 1
    for digit in digits:
        strides.extend(d * width for d in range(1, digit))
        width *= digit
    copies = len(strides)
    widths = jnp.asarray(strides, jnp.float32)[:, None, None]
    lift = jnp.exp(-decay_rate[None] * (rows * (widths - 1.0))).reshape(copies, poles, subl, LANES)
    keep = jnp.exp(-decay_rate[None] * (rows * widths)).reshape(copies, poles, subl, LANES)
    state_shape = (poles, subl, LANES)
    start = pl.pallas_call(
        functools.partial(carry_kernel, peers, digits),
        out_shape=jax.ShapeDtypeStruct(state_shape, jnp.float32),
        in_specs=vmem_specs(3),
        out_specs=pl.BlockSpec(memory_space=pltpu.VMEM),
        scratch_shapes=[
            pltpu.VMEM((len(digits),) + state_shape, jnp.float32),
            pltpu.VMEM((copies,) + state_shape, jnp.float32),
            pltpu.SemaphoreType.DMA((copies,)),
            pltpu.SemaphoreType.DMA((copies,)),
        ],
        compiler_params=pltpu.CompilerParams(collective_id=tag, has_side_effects=True),
        cost_estimate=pl.CostEstimate(
            flops=400 * rows * poles * chans, transcendentals=0, bytes_accessed=lift.size * 8
        ),
    )(end, lift, keep)
    out = pl.pallas_call(
        mixed_kernel,
        out_shape=jax.ShapeDtypeStruct((rows, subl, LANES), jnp.float32),
        in_specs=vmem_specs(6),
        out_specs=pl.BlockSpec(memory_space=pltpu.VMEM),
        cost_estimate=pl.CostEstimate(
            flops=80 * rows * poles * chans, transcendentals=0, bytes_accessed=x.size * 4
        ),
    )(x, taps, decay, resid, direct, start)
    return out.reshape(rows, chans)


def per_device(tokens, in_weight, conv_taps, decay_rate, residue, skip):
    rows = tokens.shape[0]
    chans = in_weight.shape[2]
    core = lax.axis_index("core")
    whole = gathered_tp(tokens)
    split = whole.reshape(rows, -1, 2, in_weight.shape[0])
    mine = jnp.where(core == 0, split[:, :, 0], split[:, :, 1]).reshape(rows, -1)
    theirs = jnp.where(core == 0, split[:, :, 1], split[:, :, 0]).reshape(rows, -1)
    both = jnp.concatenate([mine, swapped(theirs, "core")], axis=0)
    pieces = 2 if chans % (2 * LANES) == 0 else 1
    width = chans // pieces
    cuts = [slice(h * width, (h + 1) * width) for h in range(pieces)]
    gathered_w = [lax.all_gather(in_weight[:, :, cut], "cx", axis=0, tiled=True) for cut in cuts]
    outs = []
    for h, cut in enumerate(cuts):
        piece = gathered_w[h]
        if outs:
            piece, done = lax.optimization_barrier((piece, outs[-1]))
            outs[-1] = done
        outs.append(
            block_half(
                both, piece, conv_taps[:, :, cut], decay_rate[:, cut],
                residue[:, cut], skip[cut], rows, h,
            )
        )
    return jnp.concatenate(outs, axis=1).astype(jnp.bfloat16)


def solution(mesh):
    ctx, tp = mesh.shape["ctx"], mesh.shape["tp"]
    split = jax.sharding.Mesh(mesh.devices.reshape(ctx // 2, 2, tp), ("cx", "core", "tp"))
    c = ("cx", "core")
    placed = (
        P(c, "tp"),
        P(c, None, "tp"),
        P(None, None, "tp"),
        P(None, "tp"),
        P(None, "tp"),
        P("tp"),
    )
    return jax.shard_map(
        per_device, mesh=split, in_specs=placed, out_specs=P(c, "tp"), check_vma=False
    )
```

```python
import functools

import jax
import jax.numpy as jnp
from jax import lax
from jax.experimental import pallas as pl
from jax.experimental.pallas import tpu as pltpu
from jax.sharding import PartitionSpec as P

MESH = pl.DeviceIdType.MESH

LANES = 128


def filtered_at(x_ref, taps_ref, g, t):
    return (
        taps_ref[0, g] * x_ref[g, t + 2]
        + taps_ref[1, g] * x_ref[g, t + 1]
        + taps_ref[2, g] * x_ref[g, t]
    )


def local_end_kernel(x_ref, taps_ref, decay_ref, end_ref):
    rows = x_ref.shape[1] - 2

    def step(t, state):
        gated = filtered_at(x_ref, taps_ref, 1, t) * filtered_at(x_ref, taps_ref, 2, t)
        return decay_ref[...] * state + gated[None]

    end_ref[...] = lax.fori_loop(
        0, rows, step, jnp.zeros(end_ref.shape, jnp.float32), unroll=8
    )


def mixed_kernel(x_ref, taps_ref, decay_ref, resid_ref, skip_ref, start_ref, out_ref):
    rows = x_ref.shape[1] - 2

    def step(t, state):
        query = filtered_at(x_ref, taps_ref, 0, t)
        gated = filtered_at(x_ref, taps_ref, 1, t) * filtered_at(x_ref, taps_ref, 2, t)
        state = decay_ref[...] * state + gated[None]
        convolved = jnp.sum(resid_ref[...] * state, axis=0)
        out_ref[t] = query * (convolved + skip_ref[...] * gated)
        return state

    lax.fori_loop(0, rows, step, start_ref[...], unroll=8)


def block_kernel(
    peers, digits, x_ref, taps_ref, decay_ref, resid_ref, skip_ref, lift_ref, keep_ref, out_ref,
    end_ref, start_ref, held, slots, send_sem, recv_sem,
):
    me = lax.axis_index("cx") * 2 + lax.axis_index("core")
    tp = lax.axis_index("tp")

    def device(i):
        return (i // 2, i % 2, tp)

    steps = []
    width = 1
    for r, digit in enumerate(digits):
        steps.extend((r, d * width) for d in range(1, digit))
        width *= digit

    barrier = pltpu.get_barrier_semaphore()
    for _, by in steps:
        for peer in ((me + by) % peers, (me + peers - by) % peers):
            pl.semaphore_signal(barrier, inc=1, device_id=device(peer), device_id_type=MESH)
    local_end_kernel(x_ref, taps_ref, decay_ref, end_ref)
    pl.semaphore_wait(barrier, 2 * len(steps))

    held[0] = end_ref[...]
    start_ref[...] = jnp.zeros(start_ref.shape, jnp.float32)
    copies = []
    for r in range(len(digits)):
        mine = [(n, by) for n, (q, by) in enumerate(steps) if q == r]
        for n, by in mine:
            copy = pltpu.make_async_remote_copy(
                src_ref=held.at[r],
                dst_ref=slots.at[n],
                send_sem=send_sem.at[n],
                recv_sem=recv_sem.at[n],
                device_id=device((me + by) % peers),
                device_id_type=MESH,
            )
            copy.start()
            copies.append(copy)
        grown = held[r]
        for n, by in mine:
            copies[n].wait_recv()
            got = jnp.where(me >= by, slots[n], 0.0)
            start_ref[...] += lift_ref[n] * got
            grown = grown + keep_ref[n] * got
        if r + 1 < len(digits):
            held[r + 1] = grown
    mixed_kernel(x_ref, taps_ref, decay_ref, resid_ref, skip_ref, start_ref, out_ref)
    for copy in copies:
        copy.wait_send()


def scan_digits(peers):
    digits = []
    while peers > 1:
        digit = 4 if peers % 4 == 0 and peers != 8 else 2
        digits.append(digit)
        peers //= digit
    return digits or [2]


def vmem_specs(n):
    return [pl.BlockSpec(memory_space=pltpu.VMEM)] * n


def shifted(array, axes, by):
    peers = 1
    for axis in axes:
        peers *= lax.axis_size(axis)
    pairs = [(i, i + by) for i in range(peers) if i + by < peers]
    return lax.ppermute(array, axes, pairs)


def swapped(array, axis):
    return lax.ppermute(array, axis, [(0, 1), (1, 0)])


def gathered_tp(tokens):
    peers, here = lax.axis_size("tp"), lax.axis_index("tp")
    blocks = [tokens]
    for by in range(1, peers):
        blocks.append(lax.ppermute(tokens, "tp", [(i, (i + by) % peers) for i in range(peers)]))
    stacked = jnp.stack(blocks, axis=0)
    order = (here - jnp.arange(peers)) % peers
    placed = jnp.take(stacked, jnp.argsort(order), axis=0)
    return jnp.transpose(placed, (1, 0, 2)).reshape(tokens.shape[0], -1)


def per_device(tokens, in_weight, conv_taps, decay_rate, residue, skip):
    ctx = ("cx", "core")
    rows = tokens.shape[0]
    chans = in_weight.shape[2]
    poles = decay_rate.shape[0]
    subl = chans // LANES
    core = lax.axis_index("core")
    piece = lax.all_gather(in_weight, "cx", axis=0, tiled=True)
    whole = gathered_tp(tokens)
    split = whole.reshape(rows, -1, 2, in_weight.shape[0])
    mine = jnp.where(core == 0, split[:, :, 0], split[:, :, 1]).reshape(rows, -1)
    theirs = jnp.where(core == 0, split[:, :, 1], split[:, :, 0]).reshape(rows, -1)
    both = jnp.concatenate([mine, swapped(theirs, "core")], axis=0)
    partial = jnp.stack(
        [jnp.dot(both, piece[:, g, :], preferred_element_type=jnp.float32) for g in range(3)],
        axis=0,
    )
    sums = partial[:, :rows] + swapped(partial[:, rows:], "core")
    projected = sums.astype(jnp.bfloat16)
    edge_out = shifted(projected[:, rows - 2 :, :], ctx, 1)
    extended = jnp.concatenate([edge_out, projected], axis=1)
    values = lax.optimization_barrier(extended).astype(jnp.float32)
    x = values.reshape(3, rows + 2, subl, LANES)
    taps = conv_taps.reshape(3, 3, subl, LANES)
    decay = jnp.exp(-decay_rate).reshape(poles, subl, LANES)
    resid = residue.reshape(poles, subl, LANES)
    direct = skip.reshape(subl, LANES)

    peers = lax.axis_size("cx") * lax.axis_size("core")
    digits = scan_digits(peers)
    strides, width = [], 1
    for digit in digits:
        strides.extend(d * width for d in range(1, digit))
        width *= digit
    copies = len(strides)
    widths = jnp.asarray(strides, jnp.float32)[:, None, None]
    lift = jnp.exp(-decay_rate[None] * (rows * (widths - 1.0))).reshape(copies, poles, subl, LANES)
    keep = jnp.exp(-decay_rate[None] * (rows * widths)).reshape(copies, poles, subl, LANES)
    state_shape = (poles, subl, LANES)
    out = pl.pallas_call(
        functools.partial(block_kernel, peers, digits),
        out_shape=jax.ShapeDtypeStruct((rows, subl, LANES), jnp.float32),
        in_specs=vmem_specs(7),
        out_specs=pl.BlockSpec(memory_space=pltpu.VMEM),
        scratch_shapes=[
            pltpu.VMEM(state_shape, jnp.float32),
            pltpu.VMEM(state_shape, jnp.float32),
            pltpu.VMEM((len(digits),) + state_shape, jnp.float32),
            pltpu.VMEM((copies,) + state_shape, jnp.float32),
            pltpu.SemaphoreType.DMA((copies,)),
            pltpu.SemaphoreType.DMA((copies,)),
        ],
        compiler_params=pltpu.CompilerParams(collective_id=0, has_side_effects=True),
    )(x, taps, decay, resid, direct, lift, keep)
    return out.reshape(rows, chans).astype(jnp.bfloat16)


def solution(mesh):
    ctx, tp = mesh.shape["ctx"], mesh.shape["tp"]
    split = jax.sharding.Mesh(mesh.devices.reshape(ctx // 2, 2, tp), ("cx", "core", "tp"))
    c = ("cx", "core")
    placed = (
        P(c, "tp"),
        P(c, None, "tp"),
        P(None, None, "tp"),
        P(None, "tp"),
        P(None, "tp"),
        P("tp"),
    )
    return jax.shard_map(
        per_device, mesh=split, in_specs=placed, out_specs=P(c, "tp"), check_vma=False
    )
```

```python
import functools

import jax
import jax.numpy as jnp
from jax import lax
from jax.experimental import pallas as pl
from jax.experimental.pallas import tpu as pltpu
from jax.sharding import PartitionSpec as P

MESH = pl.DeviceIdType.MESH

LANES = 128


def filtered_at(x_ref, taps_ref, g, t):
    return (
        taps_ref[0, g] * x_ref[g, t + 2]
        + taps_ref[1, g] * x_ref[g, t + 1]
        + taps_ref[2, g] * x_ref[g, t]
    )


def local_end_kernel(x_ref, taps_ref, decay_ref, end_ref):
    rows = x_ref.shape[1] - 2

    def step(t, state):
        gated = filtered_at(x_ref, taps_ref, 1, t) * filtered_at(x_ref, taps_ref, 2, t)
        return decay_ref[...] * state + gated[None]

    end_ref[...] = lax.fori_loop(
        0, rows, step, jnp.zeros(end_ref.shape, jnp.float32), unroll=8
    )


def mixed_kernel(x_ref, taps_ref, decay_ref, resid_ref, skip_ref, start_ref, out_ref):
    rows = x_ref.shape[1] - 2

    def step(t, state):
        query = filtered_at(x_ref, taps_ref, 0, t)
        gated = filtered_at(x_ref, taps_ref, 1, t) * filtered_at(x_ref, taps_ref, 2, t)
        state = decay_ref[...] * state + gated[None]
        convolved = jnp.sum(resid_ref[...] * state, axis=0)
        out_ref[t] = query * (convolved + skip_ref[...] * gated)
        return state

    lax.fori_loop(0, rows, step, start_ref[...], unroll=8)


def block_kernel(
    peers, digits, x_ref, taps_ref, decay_ref, resid_ref, skip_ref, lift_ref, keep_ref, out_ref,
    end_ref, start_ref, held, slots, send_sem, recv_sem,
):
    me = lax.axis_index("cx") * 2 + lax.axis_index("core")
    tp = lax.axis_index("tp")

    def device(i):
        return (i // 2, i % 2, tp)

    steps = []
    width = 1
    for r, digit in enumerate(digits):
        steps.extend((r, d * width) for d in range(1, digit))
        width *= digit

    barrier = pltpu.get_barrier_semaphore()
    for _, by in steps:
        for peer in ((me + by) % peers, (me + peers - by) % peers):
            pl.semaphore_signal(barrier, inc=1, device_id=device(peer), device_id_type=MESH)
    local_end_kernel(x_ref, taps_ref, decay_ref, end_ref)
    pl.semaphore_wait(barrier, 2 * len(steps))

    held[0] = end_ref[...]
    start_ref[...] = jnp.zeros(start_ref.shape, jnp.float32)
    copies = []
    for r in range(len(digits)):
        mine = [(n, by) for n, (q, by) in enumerate(steps) if q == r]
        for n, by in mine:
            copy = pltpu.make_async_remote_copy(
                src_ref=held.at[r],
                dst_ref=slots.at[n],
                send_sem=send_sem.at[n],
                recv_sem=recv_sem.at[n],
                device_id=device((me + by) % peers),
                device_id_type=MESH,
            )
            copy.start()
            copies.append(copy)
        grown = held[r]
        for n, by in mine:
            copies[n].wait_recv()
            got = jnp.where(me >= by, slots[n], 0.0)
            start_ref[...] += lift_ref[n] * got
            grown = grown + keep_ref[n] * got
        if r + 1 < len(digits):
            held[r + 1] = grown
    mixed_kernel(x_ref, taps_ref, decay_ref, resid_ref, skip_ref, start_ref, out_ref)
    for copy in copies:
        copy.wait_send()


def scan_digits(peers):
    digits = []
    while peers > 1:
        digit = 4 if peers % 4 == 0 and peers != 8 else 2
        digits.append(digit)
        peers //= digit
    return digits or [2]


def vmem_specs(n):
    return [pl.BlockSpec(memory_space=pltpu.VMEM)] * n


def shifted(array, axes, by):
    peers = 1
    for axis in axes:
        peers *= lax.axis_size(axis)
    pairs = [(i, i + by) for i in range(peers) if i + by < peers]
    return lax.ppermute(array, axes, pairs)


def swapped(array, axis):
    return lax.ppermute(array, axis, [(0, 1), (1, 0)])


def gathered_tp(tokens):
    peers, here = lax.axis_size("tp"), lax.axis_index("tp")
    blocks = [tokens]
    for by in range(1, peers):
        blocks.append(lax.ppermute(tokens, "tp", [(i, (i + by) % peers) for i in range(peers)]))
    stacked = jnp.stack(blocks, axis=0)
    order = (here - jnp.arange(peers)) % peers
    placed = jnp.take(stacked, jnp.argsort(order), axis=0)
    return jnp.transpose(placed, (1, 0, 2)).reshape(tokens.shape[0], -1)


def per_device(tokens, in_weight, conv_taps, decay_rate, residue, skip):
    ctx = ("cx", "core")
    rows = tokens.shape[0]
    chans = in_weight.shape[2]
    poles = decay_rate.shape[0]
    subl = chans // LANES
    core = lax.axis_index("core")
    piece = lax.all_gather(in_weight, "cx", axis=0, tiled=True)
    whole = gathered_tp(tokens)
    split = whole.reshape(rows, -1, 2, in_weight.shape[0])
    mine = jnp.where(core == 0, split[:, :, 0], split[:, :, 1]).reshape(rows, -1)
    theirs = jnp.where(core == 0, split[:, :, 1], split[:, :, 0]).reshape(rows, -1)
    both = jnp.concatenate([mine, swapped(theirs, "core")], axis=0)
    taps = conv_taps.reshape(3, 3, subl, LANES)
    decay = jnp.exp(-decay_rate).reshape(poles, subl, LANES)
    resid = residue.reshape(poles, subl, LANES)
    direct = skip.reshape(subl, LANES)
    peers = lax.axis_size("cx") * lax.axis_size("core")
    digits = scan_digits(peers)
    strides, width = [], 1
    for digit in digits:
        strides.extend(d * width for d in range(1, digit))
        width *= digit
    copies = len(strides)
    widths = jnp.asarray(strides, jnp.float32)[:, None, None]
    lift = jnp.exp(-decay_rate[None] * (rows * (widths - 1.0))).reshape(copies, poles, subl, LANES)
    keep = jnp.exp(-decay_rate[None] * (rows * widths)).reshape(copies, poles, subl, LANES)
    (taps, decay, resid, direct, lift, keep), both = lax.optimization_barrier(
        ((taps, decay, resid, direct, lift, keep), both)
    )
    partial = jnp.stack(
        [jnp.dot(both, piece[:, g, :], preferred_element_type=jnp.float32) for g in range(3)],
        axis=0,
    )
    sums = partial[:, :rows] + swapped(partial[:, rows:], "core")
    projected = sums.astype(jnp.bfloat16)
    edge_out = shifted(projected[:, rows - 2 :, :], ctx, 1)
    extended = jnp.concatenate([edge_out, projected], axis=1)
    values = lax.optimization_barrier(extended).astype(jnp.float32)
    x = values.reshape(3, rows + 2, subl, LANES)
    state_shape = (poles, subl, LANES)
    out = pl.pallas_call(
        functools.partial(block_kernel, peers, digits),
        out_shape=jax.ShapeDtypeStruct((rows, subl, LANES), jnp.float32),
        in_specs=vmem_specs(7),
        out_specs=pl.BlockSpec(memory_space=pltpu.VMEM),
        scratch_shapes=[
            pltpu.VMEM(state_shape, jnp.float32),
            pltpu.VMEM(state_shape, jnp.float32),
            pltpu.VMEM((len(digits),) + state_shape, jnp.float32),
            pltpu.VMEM((copies,) + state_shape, jnp.float32),
            pltpu.SemaphoreType.DMA((copies,)),
            pltpu.SemaphoreType.DMA((copies,)),
        ],
        compiler_params=pltpu.CompilerParams(collective_id=0, has_side_effects=True),
    )(x, taps, decay, resid, direct, lift, keep)
    return out.reshape(rows, chans).astype(jnp.bfloat16)


def solution(mesh):
    ctx, tp = mesh.shape["ctx"], mesh.shape["tp"]
    split = jax.sharding.Mesh(mesh.devices.reshape(ctx // 2, 2, tp), ("cx", "core", "tp"))
    c = ("cx", "core")
    placed = (
        P(c, "tp"),
        P(c, None, "tp"),
        P(None, None, "tp"),
        P(None, "tp"),
        P(None, "tp"),
        P("tp"),
    )
    return jax.shard_map(
        per_device, mesh=split, in_specs=placed, out_specs=P(c, "tp"), check_vma=False
    )
```

```python
import functools

import jax
import jax.numpy as jnp
from jax import lax
from jax.experimental import pallas as pl
from jax.experimental.pallas import tpu as pltpu
from jax.sharding import PartitionSpec as P

MESH = pl.DeviceIdType.MESH

LANES = 128


def filtered_at(x_ref, taps_ref, g, t):
    return (
        taps_ref[0, g] * x_ref[g, t + 2]
        + taps_ref[1, g] * x_ref[g, t + 1]
        + taps_ref[2, g] * x_ref[g, t]
    )


def local_end_kernel(x_ref, taps_ref, decay_ref, end_ref):
    rows = x_ref.shape[1] - 2

    def step(t, state):
        gated = filtered_at(x_ref, taps_ref, 1, t) * filtered_at(x_ref, taps_ref, 2, t)
        return decay_ref[...] * state + gated[None]

    end_ref[...] = lax.fori_loop(
        0, rows, step, jnp.zeros(end_ref.shape, jnp.float32), unroll=8
    )


def mixed_kernel(x_ref, taps_ref, decay_ref, resid_ref, skip_ref, start_ref, out_ref):
    rows = x_ref.shape[1] - 2

    def step(t, state):
        query = filtered_at(x_ref, taps_ref, 0, t)
        gated = filtered_at(x_ref, taps_ref, 1, t) * filtered_at(x_ref, taps_ref, 2, t)
        state = decay_ref[...] * state + gated[None]
        convolved = jnp.sum(resid_ref[...] * state, axis=0)
        out_ref[t] = query * (convolved + skip_ref[...] * gated)
        return state

    lax.fori_loop(0, rows, step, start_ref[...], unroll=8)


def block_kernel(
    peers, digits, x_ref, taps_ref, decay_ref, resid_ref, skip_ref, lift_ref, keep_ref, out_ref,
    end_ref, start_ref, held, slots, send_sem, recv_sem,
):
    me = lax.axis_index("cx") * 2 + lax.axis_index("core")
    tp = lax.axis_index("tp")

    def device(i):
        return (i // 2, i % 2, tp)

    steps = []
    width = 1
    for r, digit in enumerate(digits):
        steps.extend((r, d * width) for d in range(1, digit))
        width *= digit

    barrier = pltpu.get_barrier_semaphore()
    for _, by in steps:
        for peer in ((me + by) % peers, (me + peers - by) % peers):
            pl.semaphore_signal(barrier, inc=1, device_id=device(peer), device_id_type=MESH)
    local_end_kernel(x_ref, taps_ref, decay_ref, end_ref)
    pl.semaphore_wait(barrier, 2 * len(steps))

    held[0] = end_ref[...]
    start_ref[...] = jnp.zeros(start_ref.shape, jnp.float32)
    copies = []
    for r in range(len(digits)):
        mine = [(n, by) for n, (q, by) in enumerate(steps) if q == r]
        for n, by in mine:
            copy = pltpu.make_async_remote_copy(
                src_ref=held.at[r],
                dst_ref=slots.at[n],
                send_sem=send_sem.at[n],
                recv_sem=recv_sem.at[n],
                device_id=device((me + by) % peers),
                device_id_type=MESH,
            )
            copy.start()
            copies.append(copy)
        grown = held[r]
        for n, by in mine:
            copies[n].wait_recv()
            got = jnp.where(me >= by, slots[n], 0.0)
            start_ref[...] += lift_ref[n] * got
            grown = grown + keep_ref[n] * got
        if r + 1 < len(digits):
            held[r + 1] = grown
    mixed_kernel(x_ref, taps_ref, decay_ref, resid_ref, skip_ref, start_ref, out_ref)
    for copy in copies:
        copy.wait_send()


def scan_digits(peers):
    digits = []
    while peers > 1:
        digit = 8 if peers % 8 == 0 and not digits else (4 if peers % 4 == 0 else 2)
        digits.append(digit)
        peers //= digit
    return digits or [2]


def vmem_specs(n):
    return [pl.BlockSpec(memory_space=pltpu.VMEM)] * n


def shifted(array, axes, by):
    peers = 1
    for axis in axes:
        peers *= lax.axis_size(axis)
    pairs = [(i, i + by) for i in range(peers) if i + by < peers]
    return lax.ppermute(array, axes, pairs)


def swapped(array, axis):
    return lax.ppermute(array, axis, [(0, 1), (1, 0)])


def gathered_tp(tokens):
    peers, here = lax.axis_size("tp"), lax.axis_index("tp")
    blocks = [tokens]
    for by in range(1, peers):
        blocks.append(lax.ppermute(tokens, "tp", [(i, (i + by) % peers) for i in range(peers)]))
    stacked = jnp.stack(blocks, axis=0)
    order = (here - jnp.arange(peers)) % peers
    placed = jnp.take(stacked, jnp.argsort(order), axis=0)
    return jnp.transpose(placed, (1, 0, 2)).reshape(tokens.shape[0], -1)


def per_device(tokens, in_weight, conv_taps, decay_rate, residue, skip):
    ctx = ("cx", "core")
    rows = tokens.shape[0]
    chans = in_weight.shape[2]
    poles = decay_rate.shape[0]
    subl = chans // LANES
    core = lax.axis_index("core")
    piece = lax.all_gather(in_weight, "cx", axis=0, tiled=True)
    whole = gathered_tp(tokens)
    split = whole.reshape(rows, -1, 2, in_weight.shape[0])
    mine = jnp.where(core == 0, split[:, :, 0], split[:, :, 1]).reshape(rows, -1)
    theirs = jnp.where(core == 0, split[:, :, 1], split[:, :, 0]).reshape(rows, -1)
    both = jnp.concatenate([mine, swapped(theirs, "core")], axis=0)
    taps = conv_taps.reshape(3, 3, subl, LANES)
    decay = jnp.exp(-decay_rate).reshape(poles, subl, LANES)
    resid = residue.reshape(poles, subl, LANES)
    direct = skip.reshape(subl, LANES)
    peers = lax.axis_size("cx") * lax.axis_size("core")
    digits = scan_digits(peers)
    strides, width = [], 1
    for digit in digits:
        strides.extend(d * width for d in range(1, digit))
        width *= digit
    copies = len(strides)
    widths = jnp.asarray(strides, jnp.float32)[:, None, None]
    lift = jnp.exp(-decay_rate[None] * (rows * (widths - 1.0))).reshape(copies, poles, subl, LANES)
    keep = jnp.exp(-decay_rate[None] * (rows * widths)).reshape(copies, poles, subl, LANES)
    (taps, decay, resid, direct, lift, keep), both = lax.optimization_barrier(
        ((taps, decay, resid, direct, lift, keep), both)
    )
    partial = jnp.stack(
        [jnp.dot(both, piece[:, g, :], preferred_element_type=jnp.float32) for g in range(3)],
        axis=0,
    )
    sums = partial[:, :rows] + swapped(partial[:, rows:], "core")
    projected = sums.astype(jnp.bfloat16)
    edge_out = shifted(projected[:, rows - 2 :, :], ctx, 1)
    extended = jnp.concatenate([edge_out, projected], axis=1)
    values = lax.optimization_barrier(extended).astype(jnp.float32)
    x = values.reshape(3, rows + 2, subl, LANES)
    state_shape = (poles, subl, LANES)
    out = pl.pallas_call(
        functools.partial(block_kernel, peers, digits),
        out_shape=jax.ShapeDtypeStruct((rows, subl, LANES), jnp.float32),
        in_specs=vmem_specs(7),
        out_specs=pl.BlockSpec(memory_space=pltpu.VMEM),
        scratch_shapes=[
            pltpu.VMEM(state_shape, jnp.float32),
            pltpu.VMEM(state_shape, jnp.float32),
            pltpu.VMEM((len(digits),) + state_shape, jnp.float32),
            pltpu.VMEM((copies,) + state_shape, jnp.float32),
            pltpu.SemaphoreType.DMA((copies,)),
            pltpu.SemaphoreType.DMA((copies,)),
        ],
        compiler_params=pltpu.CompilerParams(collective_id=0, has_side_effects=True),
    )(x, taps, decay, resid, direct, lift, keep)
    return out.reshape(rows, chans).astype(jnp.bfloat16)


def solution(mesh):
    ctx, tp = mesh.shape["ctx"], mesh.shape["tp"]
    split = jax.sharding.Mesh(mesh.devices.reshape(ctx // 2, 2, tp), ("cx", "core", "tp"))
    c = ("cx", "core")
    placed = (
        P(c, "tp"),
        P(c, None, "tp"),
        P(None, None, "tp"),
        P(None, "tp"),
        P(None, "tp"),
        P("tp"),
    )
    return jax.shard_map(
        per_device, mesh=split, in_specs=placed, out_specs=P(c, "tp"), check_vma=False
    )
```

```python
import functools

import jax
import jax.numpy as jnp
from jax import lax
from jax.experimental import pallas as pl
from jax.experimental.pallas import tpu as pltpu
from jax.sharding import PartitionSpec as P

MESH = pl.DeviceIdType.MESH

LANES = 128


def filtered_at(x_ref, taps_ref, g, t):
    return (
        taps_ref[0, g] * x_ref[g, t + 2]
        + taps_ref[1, g] * x_ref[g, t + 1]
        + taps_ref[2, g] * x_ref[g, t]
    )


def local_end_kernel(x_ref, taps_ref, decay_ref, end_ref):
    rows = x_ref.shape[1] - 2

    def step(t, state):
        gated = filtered_at(x_ref, taps_ref, 1, t) * filtered_at(x_ref, taps_ref, 2, t)
        return decay_ref[...] * state + gated[None]

    end_ref[...] = lax.fori_loop(
        0, rows, step, jnp.zeros(end_ref.shape, jnp.float32), unroll=8
    )


def mixed_kernel(x_ref, taps_ref, decay_ref, resid_ref, skip_ref, start_ref, out_ref):
    rows = x_ref.shape[1] - 2

    def step(t, state):
        query = filtered_at(x_ref, taps_ref, 0, t)
        gated = filtered_at(x_ref, taps_ref, 1, t) * filtered_at(x_ref, taps_ref, 2, t)
        state = decay_ref[...] * state + gated[None]
        convolved = jnp.sum(resid_ref[...] * state, axis=0)
        out_ref[t] = query * (convolved + skip_ref[...] * gated)
        return state

    lax.fori_loop(0, rows, step, start_ref[...], unroll=8)


def block_kernel(
    peers, digits, x_ref, taps_ref, decay_ref, resid_ref, skip_ref, lift_ref, keep_ref, out_ref,
    end_ref, start_ref, held, slots, send_sem, recv_sem,
):
    me = lax.axis_index("cx") * 2 + lax.axis_index("core")
    tp = lax.axis_index("tp")

    def device(i):
        return (i // 2, i % 2, tp)

    steps = []
    width = 1
    for r, digit in enumerate(digits):
        steps.extend((r, d * width) for d in range(1, digit))
        width *= digit

    barrier = pltpu.get_barrier_semaphore()
    for _, by in steps:
        for peer in ((me + by) % peers, (me + peers - by) % peers):
            pl.semaphore_signal(barrier, inc=1, device_id=device(peer), device_id_type=MESH)
    local_end_kernel(x_ref, taps_ref, decay_ref, end_ref)
    pl.semaphore_wait(barrier, 2 * len(steps))

    held[0] = end_ref[...]
    start_ref[...] = jnp.zeros(start_ref.shape, jnp.float32)
    copies = []
    for r in range(len(digits)):
        mine = [(n, by) for n, (q, by) in enumerate(steps) if q == r]
        for n, by in mine:
            copy = pltpu.make_async_remote_copy(
                src_ref=held.at[r],
                dst_ref=slots.at[n],
                send_sem=send_sem.at[n],
                recv_sem=recv_sem.at[n],
                device_id=device((me + by) % peers),
                device_id_type=MESH,
            )
            copy.start()
            copies.append(copy)
        grown = held[r]
        for n, by in mine:
            copies[n].wait_recv()
            got = jnp.where(me >= by, slots[n], 0.0)
            start_ref[...] += lift_ref[n] * got
            grown = grown + keep_ref[n] * got
        if r + 1 < len(digits):
            held[r + 1] = grown
    mixed_kernel(x_ref, taps_ref, decay_ref, resid_ref, skip_ref, start_ref, out_ref)
    for copy in copies:
        copy.wait_send()


def scan_digits(peers):
    digits = []
    while peers > 1:
        digit = 4 if peers % 4 == 0 and peers != 8 else 2
        digits.append(digit)
        peers //= digit
    return digits or [2]


def vmem_specs(n):
    return [pl.BlockSpec(memory_space=pltpu.VMEM)] * n


def shifted(array, axes, by):
    peers = 1
    for axis in axes:
        peers *= lax.axis_size(axis)
    pairs = [(i, i + by) for i in range(peers) if i + by < peers]
    return lax.ppermute(array, axes, pairs)


def swapped(array, axis):
    return lax.ppermute(array, axis, [(0, 1), (1, 0)])


def gathered_tp(tokens):
    peers, here = lax.axis_size("tp"), lax.axis_index("tp")
    blocks = [tokens]
    for by in range(1, peers):
        blocks.append(lax.ppermute(tokens, "tp", [(i, (i + by) % peers) for i in range(peers)]))
    stacked = jnp.stack(blocks, axis=0)
    order = (here - jnp.arange(peers)) % peers
    placed = jnp.take(stacked, jnp.argsort(order), axis=0)
    return jnp.transpose(placed, (1, 0, 2)).reshape(tokens.shape[0], -1)


def per_device(tokens, in_weight, conv_taps, decay_rate, residue, skip):
    ctx = ("cx", "core")
    rows = tokens.shape[0]
    chans = in_weight.shape[2]
    poles = decay_rate.shape[0]
    subl = chans // LANES
    core = lax.axis_index("core")
    piece = lax.all_gather(in_weight, "cx", axis=0, tiled=True)
    whole = gathered_tp(tokens)
    split = whole.reshape(rows, -1, 2, in_weight.shape[0])
    mine = jnp.where(core == 0, split[:, :, 0], split[:, :, 1]).reshape(rows, -1)
    theirs = jnp.where(core == 0, split[:, :, 1], split[:, :, 0]).reshape(rows, -1)
    both = jnp.concatenate([mine, swapped(theirs, "core")], axis=0)
    taps = conv_taps.reshape(3, 3, subl, LANES)
    decay = jnp.exp(-decay_rate).reshape(poles, subl, LANES)
    resid = residue.reshape(poles, subl, LANES)
    direct = skip.reshape(subl, LANES)
    peers = lax.axis_size("cx") * lax.axis_size("core")
    digits = scan_digits(peers)
    strides, width = [], 1
    for digit in digits:
        strides.extend(d * width for d in range(1, digit))
        width *= digit
    copies = len(strides)
    widths = jnp.asarray(strides, jnp.float32)[:, None, None]
    lift = jnp.exp(-decay_rate[None] * (rows * (widths - 1.0))).reshape(copies, poles, subl, LANES)
    keep = jnp.exp(-decay_rate[None] * (rows * widths)).reshape(copies, poles, subl, LANES)
    (taps, decay, resid, direct, lift, keep), both = lax.optimization_barrier(
        ((taps, decay, resid, direct, lift, keep), both)
    )
    theirs_part = jnp.stack(
        [jnp.dot(both[rows:], piece[:, g, :], preferred_element_type=jnp.float32) for g in range(3)],
        axis=0,
    )
    arrived = swapped(theirs_part, "core")
    mine_part = jnp.stack(
        [jnp.dot(both[:rows], piece[:, g, :], preferred_element_type=jnp.float32) for g in range(3)],
        axis=0,
    )
    sums = mine_part + arrived
    projected = sums.astype(jnp.bfloat16)
    edge_out = shifted(projected[:, rows - 2 :, :], ctx, 1)
    extended = jnp.concatenate([edge_out, projected], axis=1)
    values = lax.optimization_barrier(extended).astype(jnp.float32)
    x = values.reshape(3, rows + 2, subl, LANES)
    state_shape = (poles, subl, LANES)
    out = pl.pallas_call(
        functools.partial(block_kernel, peers, digits),
        out_shape=jax.ShapeDtypeStruct((rows, subl, LANES), jnp.float32),
        in_specs=vmem_specs(7),
        out_specs=pl.BlockSpec(memory_space=pltpu.VMEM),
        scratch_shapes=[
            pltpu.VMEM(state_shape, jnp.float32),
            pltpu.VMEM(state_shape, jnp.float32),
            pltpu.VMEM((len(digits),) + state_shape, jnp.float32),
            pltpu.VMEM((copies,) + state_shape, jnp.float32),
            pltpu.SemaphoreType.DMA((copies,)),
            pltpu.SemaphoreType.DMA((copies,)),
        ],
        compiler_params=pltpu.CompilerParams(collective_id=0, has_side_effects=True),
    )(x, taps, decay, resid, direct, lift, keep)
    return out.reshape(rows, chans).astype(jnp.bfloat16)


def solution(mesh):
    ctx, tp = mesh.shape["ctx"], mesh.shape["tp"]
    split = jax.sharding.Mesh(mesh.devices.reshape(ctx // 2, 2, tp), ("cx", "core", "tp"))
    c = ("cx", "core")
    placed = (
        P(c, "tp"),
        P(c, None, "tp"),
        P(None, None, "tp"),
        P(None, "tp"),
        P(None, "tp"),
        P("tp"),
    )
    return jax.shard_map(
        per_device, mesh=split, in_specs=placed, out_specs=P(c, "tp"), check_vma=False
    )
```

```python
import functools

import jax
import jax.numpy as jnp
from jax import lax
from jax.experimental import pallas as pl
from jax.experimental.pallas import tpu as pltpu
from jax.sharding import PartitionSpec as P

MESH = pl.DeviceIdType.MESH

LANES = 128


def filtered_at(x_ref, taps_ref, g, t):
    return (
        taps_ref[0, g] * x_ref[g, t + 2]
        + taps_ref[1, g] * x_ref[g, t + 1]
        + taps_ref[2, g] * x_ref[g, t]
    )


def local_end_kernel(x_ref, taps_ref, decay_ref, end_ref):
    rows = x_ref.shape[1] - 2

    def step(t, state):
        gated = filtered_at(x_ref, taps_ref, 1, t) * filtered_at(x_ref, taps_ref, 2, t)
        return decay_ref[...] * state + gated[None]

    end_ref[...] = lax.fori_loop(
        0, rows, step, jnp.zeros(end_ref.shape, jnp.float32), unroll=8
    )


def mixed_kernel(x_ref, taps_ref, decay_ref, resid_ref, skip_ref, start_ref, out_ref):
    rows = x_ref.shape[1] - 2

    def step(t, state):
        query = filtered_at(x_ref, taps_ref, 0, t)
        gated = filtered_at(x_ref, taps_ref, 1, t) * filtered_at(x_ref, taps_ref, 2, t)
        state = decay_ref[...] * state + gated[None]
        convolved = jnp.sum(resid_ref[...] * state, axis=0)
        out_ref[t] = query * (convolved + skip_ref[...] * gated)
        return state

    lax.fori_loop(0, rows, step, start_ref[...], unroll=8)


def block_kernel(
    peers, digits, x_ref, taps_ref, decay_ref, resid_ref, skip_ref, lift_ref, keep_ref, out_ref,
    end_ref, start_ref, held, slots, send_sem, recv_sem,
):
    me = lax.axis_index("cx") * 2 + lax.axis_index("core")
    tp = lax.axis_index("tp")

    def device(i):
        return (i // 2, i % 2, tp)

    steps = []
    width = 1
    for r, digit in enumerate(digits):
        steps.extend((r, d * width) for d in range(1, digit))
        width *= digit

    barrier = pltpu.get_barrier_semaphore()
    for _, by in steps:
        for peer in ((me + by) % peers, (me + peers - by) % peers):
            pl.semaphore_signal(barrier, inc=1, device_id=device(peer), device_id_type=MESH)
    local_end_kernel(x_ref, taps_ref, decay_ref, end_ref)
    pl.semaphore_wait(barrier, 2 * len(steps))

    held[0] = end_ref[...]
    start_ref[...] = jnp.zeros(start_ref.shape, jnp.float32)
    copies = []
    for r in range(len(digits)):
        mine = [(n, by) for n, (q, by) in enumerate(steps) if q == r]
        for n, by in mine:
            copy = pltpu.make_async_remote_copy(
                src_ref=held.at[r],
                dst_ref=slots.at[n],
                send_sem=send_sem.at[n],
                recv_sem=recv_sem.at[n],
                device_id=device((me + by) % peers),
                device_id_type=MESH,
            )
            copy.start()
            copies.append(copy)
        grown = held[r]
        for n, by in mine:
            copies[n].wait_recv()
            got = jnp.where(me >= by, slots[n], 0.0)
            start_ref[...] += lift_ref[n] * got
            grown = grown + keep_ref[n] * got
        if r + 1 < len(digits):
            held[r + 1] = grown
    mixed_kernel(x_ref, taps_ref, decay_ref, resid_ref, skip_ref, start_ref, out_ref)
    for copy in copies:
        copy.wait_send()


def scan_digits(peers):
    digits = []
    while peers > 1:
        digit = 4 if peers % 4 == 0 and peers != 8 else 2
        digits.append(digit)
        peers //= digit
    return digits or [2]


def matmul_kernel(a_ref, w_ref, o_ref):
    o_ref[...] = jnp.dot(a_ref[...], w_ref[...], preferred_element_type=jnp.float32)


def stream_matmul(a, w, g):
    m, k = a.shape
    n = w.shape[2]
    tn = 512 if n % 512 == 0 else n
    return pl.pallas_call(
        matmul_kernel,
        out_shape=jax.ShapeDtypeStruct((m, n), jnp.float32),
        grid=(n // tn,),
        in_specs=[
            pl.BlockSpec((m, k), lambda j: (0, 0)),
            pl.BlockSpec((None, k, tn), lambda j: (g, 0, j)),
        ],
        out_specs=pl.BlockSpec((m, tn), lambda j: (0, j)),
        cost_estimate=pl.CostEstimate(
            flops=2 * m * k * n, transcendentals=0, bytes_accessed=2 * (m * k + k * n) + 4 * m * n
        ),
    )(a, w)


def vmem_specs(n):
    return [pl.BlockSpec(memory_space=pltpu.VMEM)] * n


def shifted(array, axes, by):
    peers = 1
    for axis in axes:
        peers *= lax.axis_size(axis)
    pairs = [(i, i + by) for i in range(peers) if i + by < peers]
    return lax.ppermute(array, axes, pairs)


def swapped(array, axis):
    return lax.ppermute(array, axis, [(0, 1), (1, 0)])


def gathered_tp(tokens):
    peers, here = lax.axis_size("tp"), lax.axis_index("tp")
    blocks = [tokens]
    for by in range(1, peers):
        blocks.append(lax.ppermute(tokens, "tp", [(i, (i + by) % peers) for i in range(peers)]))
    stacked = jnp.stack(blocks, axis=0)
    order = (here - jnp.arange(peers)) % peers
    placed = jnp.take(stacked, jnp.argsort(order), axis=0)
    return jnp.transpose(placed, (1, 0, 2)).reshape(tokens.shape[0], -1)


def per_device(tokens, in_weight, conv_taps, decay_rate, residue, skip):
    ctx = ("cx", "core")
    rows = tokens.shape[0]
    chans = in_weight.shape[2]
    poles = decay_rate.shape[0]
    subl = chans // LANES
    core = lax.axis_index("core")
    piece = lax.all_gather(in_weight, "cx", axis=0, tiled=True)
    whole = gathered_tp(tokens)
    split = whole.reshape(rows, -1, 2, in_weight.shape[0])
    mine = jnp.where(core == 0, split[:, :, 0], split[:, :, 1]).reshape(rows, -1)
    theirs = jnp.where(core == 0, split[:, :, 1], split[:, :, 0]).reshape(rows, -1)
    both = jnp.concatenate([mine, swapped(theirs, "core")], axis=0)
    taps = conv_taps.reshape(3, 3, subl, LANES)
    decay = jnp.exp(-decay_rate).reshape(poles, subl, LANES)
    resid = residue.reshape(poles, subl, LANES)
    direct = skip.reshape(subl, LANES)
    peers = lax.axis_size("cx") * lax.axis_size("core")
    digits = scan_digits(peers)
    strides, width = [], 1
    for digit in digits:
        strides.extend(d * width for d in range(1, digit))
        width *= digit
    copies = len(strides)
    widths = jnp.asarray(strides, jnp.float32)[:, None, None]
    lift = jnp.exp(-decay_rate[None] * (rows * (widths - 1.0))).reshape(copies, poles, subl, LANES)
    keep = jnp.exp(-decay_rate[None] * (rows * widths)).reshape(copies, poles, subl, LANES)
    (taps, decay, resid, direct, lift, keep), both = lax.optimization_barrier(
        ((taps, decay, resid, direct, lift, keep), both)
    )
    streams = jnp.transpose(piece, (1, 0, 2))
    arrived, mine_part = [], []
    for g in range(3):
        part = stream_matmul(both, streams, g)
        arrived.append(swapped(part[rows:], "core"))
        mine_part.append(part[:rows])
    arrived = jnp.stack(arrived, axis=0)
    mine_part = jnp.stack(mine_part, axis=0)
    sums = mine_part + arrived
    projected = sums.astype(jnp.bfloat16)
    edge_out = shifted(projected[:, rows - 2 :, :], ctx, 1)
    extended = jnp.concatenate([edge_out, projected], axis=1)
    values = lax.optimization_barrier(extended).astype(jnp.float32)
    x = values.reshape(3, rows + 2, subl, LANES)
    state_shape = (poles, subl, LANES)
    out = pl.pallas_call(
        functools.partial(block_kernel, peers, digits),
        out_shape=jax.ShapeDtypeStruct((rows, subl, LANES), jnp.float32),
        in_specs=vmem_specs(7),
        out_specs=pl.BlockSpec(memory_space=pltpu.VMEM),
        scratch_shapes=[
            pltpu.VMEM(state_shape, jnp.float32),
            pltpu.VMEM(state_shape, jnp.float32),
            pltpu.VMEM((len(digits),) + state_shape, jnp.float32),
            pltpu.VMEM((copies,) + state_shape, jnp.float32),
            pltpu.SemaphoreType.DMA((copies,)),
            pltpu.SemaphoreType.DMA((copies,)),
        ],
        compiler_params=pltpu.CompilerParams(collective_id=0, has_side_effects=True),
    )(x, taps, decay, resid, direct, lift, keep)
    return out.reshape(rows, chans).astype(jnp.bfloat16)


def solution(mesh):
    ctx, tp = mesh.shape["ctx"], mesh.shape["tp"]
    split = jax.sharding.Mesh(mesh.devices.reshape(ctx // 2, 2, tp), ("cx", "core", "tp"))
    c = ("cx", "core")
    placed = (
        P(c, "tp"),
        P(c, None, "tp"),
        P(None, None, "tp"),
        P(None, "tp"),
        P(None, "tp"),
        P("tp"),
    )
    return jax.shard_map(
        per_device, mesh=split, in_specs=placed, out_specs=P(c, "tp"), check_vma=False
    )
```

```python
import functools

import jax
import jax.numpy as jnp
from jax import lax
from jax.experimental import pallas as pl
from jax.experimental.pallas import tpu as pltpu
from jax.sharding import PartitionSpec as P

MESH = pl.DeviceIdType.MESH

LANES = 128


def filtered_at(x_ref, taps_ref, g, t):
    return (
        taps_ref[0, g] * x_ref[g, t + 2]
        + taps_ref[1, g] * x_ref[g, t + 1]
        + taps_ref[2, g] * x_ref[g, t]
    )


def local_end_kernel(x_ref, taps_ref, decay_ref, end_ref):
    rows = x_ref.shape[1] - 2

    def step(t, state):
        gated = filtered_at(x_ref, taps_ref, 1, t) * filtered_at(x_ref, taps_ref, 2, t)
        return decay_ref[...] * state + gated[None]

    end_ref[...] = lax.fori_loop(
        0, rows, step, jnp.zeros(end_ref.shape, jnp.float32), unroll=8
    )


def mixed_kernel(x_ref, taps_ref, decay_ref, resid_ref, skip_ref, start_ref, out_ref):
    rows = x_ref.shape[1] - 2

    def step(t, state):
        query = filtered_at(x_ref, taps_ref, 0, t)
        gated = filtered_at(x_ref, taps_ref, 1, t) * filtered_at(x_ref, taps_ref, 2, t)
        state = decay_ref[...] * state + gated[None]
        convolved = jnp.sum(resid_ref[...] * state, axis=0)
        out_ref[t] = query * (convolved + skip_ref[...] * gated)
        return state

    lax.fori_loop(0, rows, step, start_ref[...], unroll=8)


def block_kernel(
    peers, digits, x_ref, taps_ref, decay_ref, resid_ref, skip_ref, lift_ref, keep_ref, out_ref,
    end_ref, start_ref, held, slots, send_sem, recv_sem,
):
    me = lax.axis_index("cx") * 2 + lax.axis_index("core")
    tp = lax.axis_index("tp")

    def device(i):
        return (i // 2, i % 2, tp)

    steps = []
    width = 1
    for r, digit in enumerate(digits):
        steps.extend((r, d * width) for d in range(1, digit))
        width *= digit

    barrier = pltpu.get_barrier_semaphore()
    for _, by in steps:
        for peer in ((me + by) % peers, (me + peers - by) % peers):
            pl.semaphore_signal(barrier, inc=1, device_id=device(peer), device_id_type=MESH)
    local_end_kernel(x_ref, taps_ref, decay_ref, end_ref)
    pl.semaphore_wait(barrier, 2 * len(steps))

    held[0] = end_ref[...]
    start_ref[...] = jnp.zeros(start_ref.shape, jnp.float32)
    copies = []
    for r in range(len(digits)):
        mine = [(n, by) for n, (q, by) in enumerate(steps) if q == r]
        for n, by in mine:
            copy = pltpu.make_async_remote_copy(
                src_ref=held.at[r],
                dst_ref=slots.at[n],
                send_sem=send_sem.at[n],
                recv_sem=recv_sem.at[n],
                device_id=device((me + by) % peers),
                device_id_type=MESH,
            )
            copy.start()
            copies.append(copy)
        grown = held[r]
        for n, by in mine:
            copies[n].wait_recv()
            got = jnp.where(me >= by, slots[n], 0.0)
            start_ref[...] += lift_ref[n] * got
            grown = grown + keep_ref[n] * got
        if r + 1 < len(digits):
            held[r + 1] = grown
    mixed_kernel(x_ref, taps_ref, decay_ref, resid_ref, skip_ref, start_ref, out_ref)
    for copy in copies:
        copy.wait_send()


def scan_digits(peers):
    digits = []
    while peers > 1:
        digit = 4 if peers % 4 == 0 and peers != 8 else 2
        digits.append(digit)
        peers //= digit
    return digits or [2]


def matmul_kernel(a_ref, w_ref, o_ref):
    k = pl.program_id(1)
    tk = w_ref.shape[0]

    @pl.when(k == 0)
    def _():
        o_ref[...] = jnp.zeros(o_ref.shape, jnp.float32)

    cols = pl.ds(pl.multiple_of(k * tk, tk), tk)
    o_ref[...] += jnp.dot(a_ref[:, cols], w_ref[...], preferred_element_type=jnp.float32)


def stream_matmul(a, w):
    m, depth = a.shape
    streams, _, n = w.shape
    tk = 512 if depth % 512 == 0 else depth
    return pl.pallas_call(
        matmul_kernel,
        out_shape=jax.ShapeDtypeStruct((streams, m, n), jnp.float32),
        grid=(streams, depth // tk),
        in_specs=[
            pl.BlockSpec((m, depth), lambda g, k: (0, 0)),
            pl.BlockSpec((None, tk, n), lambda g, k: (g, k, 0)),
        ],
        out_specs=pl.BlockSpec((None, m, n), lambda g, k: (g, 0, 0)),
        cost_estimate=pl.CostEstimate(
            flops=2 * m * depth * n * streams,
            transcendentals=0,
            bytes_accessed=2 * (m * depth + depth * n * streams) + 4 * m * n * streams,
        ),
    )(a, w)


def vmem_specs(n):
    return [pl.BlockSpec(memory_space=pltpu.VMEM)] * n


def shifted(array, axes, by):
    peers = 1
    for axis in axes:
        peers *= lax.axis_size(axis)
    pairs = [(i, i + by) for i in range(peers) if i + by < peers]
    return lax.ppermute(array, axes, pairs)


def swapped(array, axis):
    return lax.ppermute(array, axis, [(0, 1), (1, 0)])


def gathered_tp(tokens):
    peers, here = lax.axis_size("tp"), lax.axis_index("tp")
    blocks = [tokens]
    for by in range(1, peers):
        blocks.append(lax.ppermute(tokens, "tp", [(i, (i + by) % peers) for i in range(peers)]))
    stacked = jnp.stack(blocks, axis=0)
    order = (here - jnp.arange(peers)) % peers
    placed = jnp.take(stacked, jnp.argsort(order), axis=0)
    return jnp.transpose(placed, (1, 0, 2)).reshape(tokens.shape[0], -1)


def per_device(tokens, in_weight, conv_taps, decay_rate, residue, skip):
    ctx = ("cx", "core")
    rows = tokens.shape[0]
    chans = in_weight.shape[2]
    poles = decay_rate.shape[0]
    subl = chans // LANES
    core = lax.axis_index("core")
    piece = lax.all_gather(in_weight, "cx", axis=0, tiled=True)
    whole = gathered_tp(tokens)
    split = whole.reshape(rows, -1, 2, in_weight.shape[0])
    mine = jnp.where(core == 0, split[:, :, 0], split[:, :, 1]).reshape(rows, -1)
    theirs = jnp.where(core == 0, split[:, :, 1], split[:, :, 0]).reshape(rows, -1)
    both = jnp.concatenate([mine, swapped(theirs, "core")], axis=0)
    taps = conv_taps.reshape(3, 3, subl, LANES)
    decay = jnp.exp(-decay_rate).reshape(poles, subl, LANES)
    resid = residue.reshape(poles, subl, LANES)
    direct = skip.reshape(subl, LANES)
    peers = lax.axis_size("cx") * lax.axis_size("core")
    digits = scan_digits(peers)
    strides, width = [], 1
    for digit in digits:
        strides.extend(d * width for d in range(1, digit))
        width *= digit
    copies = len(strides)
    widths = jnp.asarray(strides, jnp.float32)[:, None, None]
    lift = jnp.exp(-decay_rate[None] * (rows * (widths - 1.0))).reshape(copies, poles, subl, LANES)
    keep = jnp.exp(-decay_rate[None] * (rows * widths)).reshape(copies, poles, subl, LANES)
    (taps, decay, resid, direct, lift, keep), both = lax.optimization_barrier(
        ((taps, decay, resid, direct, lift, keep), both)
    )
    part = stream_matmul(both, jnp.transpose(piece, (1, 0, 2)))
    arrived = swapped(part[:, rows:], "core")
    mine_part = part[:, :rows]
    sums = mine_part + arrived
    projected = sums.astype(jnp.bfloat16)
    edge_out = shifted(projected[:, rows - 2 :, :], ctx, 1)
    extended = jnp.concatenate([edge_out, projected], axis=1)
    values = lax.optimization_barrier(extended).astype(jnp.float32)
    x = values.reshape(3, rows + 2, subl, LANES)
    state_shape = (poles, subl, LANES)
    out = pl.pallas_call(
        functools.partial(block_kernel, peers, digits),
        out_shape=jax.ShapeDtypeStruct((rows, subl, LANES), jnp.float32),
        in_specs=vmem_specs(7),
        out_specs=pl.BlockSpec(memory_space=pltpu.VMEM),
        scratch_shapes=[
            pltpu.VMEM(state_shape, jnp.float32),
            pltpu.VMEM(state_shape, jnp.float32),
            pltpu.VMEM((len(digits),) + state_shape, jnp.float32),
            pltpu.VMEM((copies,) + state_shape, jnp.float32),
            pltpu.SemaphoreType.DMA((copies,)),
            pltpu.SemaphoreType.DMA((copies,)),
        ],
        compiler_params=pltpu.CompilerParams(collective_id=0, has_side_effects=True),
    )(x, taps, decay, resid, direct, lift, keep)
    return out.reshape(rows, chans).astype(jnp.bfloat16)


def solution(mesh):
    ctx, tp = mesh.shape["ctx"], mesh.shape["tp"]
    split = jax.sharding.Mesh(mesh.devices.reshape(ctx // 2, 2, tp), ("cx", "core", "tp"))
    c = ("cx", "core")
    placed = (
        P(c, "tp"),
        P(c, None, "tp"),
        P(None, None, "tp"),
        P(None, "tp"),
        P(None, "tp"),
        P("tp"),
    )
    return jax.shard_map(
        per_device, mesh=split, in_specs=placed, out_specs=P(c, "tp"), check_vma=False
    )
```

```python
import functools

import jax
import jax.numpy as jnp
from jax import lax
from jax.experimental import pallas as pl
from jax.experimental.pallas import tpu as pltpu
from jax.sharding import PartitionSpec as P

MESH = pl.DeviceIdType.MESH

LANES = 128


def filtered_at(x_ref, taps_ref, g, t):
    return (
        taps_ref[0, g] * x_ref[g, t + 2]
        + taps_ref[1, g] * x_ref[g, t + 1]
        + taps_ref[2, g] * x_ref[g, t]
    )


def local_end_kernel(x_ref, taps_ref, decay_ref, end_ref):
    rows = x_ref.shape[1] - 2

    def step(t, state):
        gated = filtered_at(x_ref, taps_ref, 1, t) * filtered_at(x_ref, taps_ref, 2, t)
        return decay_ref[...] * state + gated[None]

    end_ref[...] = lax.fori_loop(
        0, rows, step, jnp.zeros(end_ref.shape, jnp.float32), unroll=8
    )


def mixed_kernel(x_ref, taps_ref, decay_ref, resid_ref, skip_ref, start_ref, out_ref):
    rows = x_ref.shape[1] - 2

    def step(t, state):
        query = filtered_at(x_ref, taps_ref, 0, t)
        gated = filtered_at(x_ref, taps_ref, 1, t) * filtered_at(x_ref, taps_ref, 2, t)
        state = decay_ref[...] * state + gated[None]
        convolved = jnp.sum(resid_ref[...] * state, axis=0)
        out_ref[t] = query * (convolved + skip_ref[...] * gated)
        return state

    lax.fori_loop(0, rows, step, start_ref[...], unroll=8)


def block_kernel(
    peers, digits, x_ref, taps_ref, decay_ref, resid_ref, skip_ref, lift_ref, keep_ref, out_ref,
    end_ref, start_ref, held, slots, send_sem, recv_sem,
):
    me = lax.axis_index("cx") * 2 + lax.axis_index("core")
    tp = lax.axis_index("tp")

    def device(i):
        return (i // 2, i % 2, tp)

    steps = []
    width = 1
    for r, digit in enumerate(digits):
        steps.extend((r, d * width) for d in range(1, digit))
        width *= digit

    barrier = pltpu.get_barrier_semaphore()
    for _, by in steps:
        for peer in ((me + by) % peers, (me + peers - by) % peers):
            pl.semaphore_signal(barrier, inc=1, device_id=device(peer), device_id_type=MESH)
    local_end_kernel(x_ref, taps_ref, decay_ref, end_ref)
    pl.semaphore_wait(barrier, 2 * len(steps))

    held[0] = end_ref[...]
    start_ref[...] = jnp.zeros(start_ref.shape, jnp.float32)
    copies = []
    for r in range(len(digits)):
        mine = [(n, by) for n, (q, by) in enumerate(steps) if q == r]
        for n, by in mine:
            copy = pltpu.make_async_remote_copy(
                src_ref=held.at[r],
                dst_ref=slots.at[n],
                send_sem=send_sem.at[n],
                recv_sem=recv_sem.at[n],
                device_id=device((me + by) % peers),
                device_id_type=MESH,
            )
            copy.start()
            copies.append(copy)
        grown = held[r]
        for n, by in mine:
            copies[n].wait_recv()
            got = jnp.where(me >= by, slots[n], 0.0)
            start_ref[...] += lift_ref[n] * got
            grown = grown + keep_ref[n] * got
        if r + 1 < len(digits):
            held[r + 1] = grown
    mixed_kernel(x_ref, taps_ref, decay_ref, resid_ref, skip_ref, start_ref, out_ref)
    for copy in copies:
        copy.wait_send()


def scan_digits(peers):
    digits = [2] if peers % 2 == 0 else []
    peers //= 2 if digits else 1
    while peers > 1:
        digit = 4 if peers % 4 == 0 else 2
        digits.append(digit)
        peers //= digit
    return digits or [2]


def vmem_specs(n):
    return [pl.BlockSpec(memory_space=pltpu.VMEM)] * n


def shifted(array, axes, by):
    peers = 1
    for axis in axes:
        peers *= lax.axis_size(axis)
    pairs = [(i, i + by) for i in range(peers) if i + by < peers]
    return lax.ppermute(array, axes, pairs)


def swapped(array, axis):
    return lax.ppermute(array, axis, [(0, 1), (1, 0)])


def gathered_tp(tokens):
    peers, here = lax.axis_size("tp"), lax.axis_index("tp")
    blocks = [tokens]
    for by in range(1, peers):
        blocks.append(lax.ppermute(tokens, "tp", [(i, (i + by) % peers) for i in range(peers)]))
    stacked = jnp.stack(blocks, axis=0)
    order = (here - jnp.arange(peers)) % peers
    placed = jnp.take(stacked, jnp.argsort(order), axis=0)
    return jnp.transpose(placed, (1, 0, 2)).reshape(tokens.shape[0], -1)


def per_device(tokens, in_weight, conv_taps, decay_rate, residue, skip):
    ctx = ("cx", "core")
    rows = tokens.shape[0]
    chans = in_weight.shape[2]
    poles = decay_rate.shape[0]
    subl = chans // LANES
    core = lax.axis_index("core")
    piece = lax.all_gather(in_weight, "cx", axis=0, tiled=True)
    whole = gathered_tp(tokens)
    split = whole.reshape(rows, -1, 2, in_weight.shape[0])
    mine = jnp.where(core == 0, split[:, :, 0], split[:, :, 1]).reshape(rows, -1)
    theirs = jnp.where(core == 0, split[:, :, 1], split[:, :, 0]).reshape(rows, -1)
    both = jnp.concatenate([mine, swapped(theirs, "core")], axis=0)
    taps = conv_taps.reshape(3, 3, subl, LANES)
    decay = jnp.exp(-decay_rate).reshape(poles, subl, LANES)
    resid = residue.reshape(poles, subl, LANES)
    direct = skip.reshape(subl, LANES)
    peers = lax.axis_size("cx") * lax.axis_size("core")
    digits = scan_digits(peers)
    strides, width = [], 1
    for digit in digits:
        strides.extend(d * width for d in range(1, digit))
        width *= digit
    copies = len(strides)
    widths = jnp.asarray(strides, jnp.float32)[:, None, None]
    lift = jnp.exp(-decay_rate[None] * (rows * (widths - 1.0))).reshape(copies, poles, subl, LANES)
    keep = jnp.exp(-decay_rate[None] * (rows * widths)).reshape(copies, poles, subl, LANES)
    (taps, decay, resid, direct, lift, keep), both = lax.optimization_barrier(
        ((taps, decay, resid, direct, lift, keep), both)
    )
    theirs_part = jnp.stack(
        [jnp.dot(both[rows:], piece[:, g, :], preferred_element_type=jnp.float32) for g in range(3)],
        axis=0,
    )
    arrived = swapped(theirs_part, "core")
    mine_part = jnp.stack(
        [jnp.dot(both[:rows], piece[:, g, :], preferred_element_type=jnp.float32) for g in range(3)],
        axis=0,
    )
    sums = mine_part + arrived
    projected = sums.astype(jnp.bfloat16)
    edge_out = shifted(projected[:, rows - 2 :, :], ctx, 1)
    extended = jnp.concatenate([edge_out, projected], axis=1)
    values = lax.optimization_barrier(extended).astype(jnp.float32)
    x = values.reshape(3, rows + 2, subl, LANES)
    state_shape = (poles, subl, LANES)
    out = pl.pallas_call(
        functools.partial(block_kernel, peers, digits),
        out_shape=jax.ShapeDtypeStruct((rows, subl, LANES), jnp.float32),
        in_specs=vmem_specs(7),
        out_specs=pl.BlockSpec(memory_space=pltpu.VMEM),
        scratch_shapes=[
            pltpu.VMEM(state_shape, jnp.float32),
            pltpu.VMEM(state_shape, jnp.float32),
            pltpu.VMEM((len(digits),) + state_shape, jnp.float32),
            pltpu.VMEM((copies,) + state_shape, jnp.float32),
            pltpu.SemaphoreType.DMA((copies,)),
            pltpu.SemaphoreType.DMA((copies,)),
        ],
        compiler_params=pltpu.CompilerParams(collective_id=0, has_side_effects=True),
    )(x, taps, decay, resid, direct, lift, keep)
    return out.reshape(rows, chans).astype(jnp.bfloat16)


def solution(mesh):
    ctx, tp = mesh.shape["ctx"], mesh.shape["tp"]
    split = jax.sharding.Mesh(mesh.devices.reshape(ctx // 2, 2, tp), ("cx", "core", "tp"))
    c = ("cx", "core")
    placed = (
        P(c, "tp"),
        P(c, None, "tp"),
        P(None, None, "tp"),
        P(None, "tp"),
        P(None, "tp"),
        P("tp"),
    )
    return jax.shard_map(
        per_device, mesh=split, in_specs=placed, out_specs=P(c, "tp"), check_vma=False
    )
```

```python
import functools

import jax
import jax.numpy as jnp
from jax import lax
from jax.experimental import pallas as pl
from jax.experimental.pallas import tpu as pltpu
from jax.sharding import PartitionSpec as P

MESH = pl.DeviceIdType.MESH

LANES = 128


def filtered_at(x_ref, taps_ref, g, t):
    return (
        taps_ref[0, g] * x_ref[g, t + 2]
        + taps_ref[1, g] * x_ref[g, t + 1]
        + taps_ref[2, g] * x_ref[g, t]
    )


def local_end_kernel(x_ref, taps_ref, decay_ref, end_ref):
    rows = x_ref.shape[1] - 2

    def step(t, state):
        gated = filtered_at(x_ref, taps_ref, 1, t) * filtered_at(x_ref, taps_ref, 2, t)
        return decay_ref[...] * state + gated[None]

    end_ref[...] = lax.fori_loop(
        0, rows, step, jnp.zeros(end_ref.shape, jnp.float32), unroll=8
    )


def mixed_kernel(x_ref, taps_ref, decay_ref, resid_ref, skip_ref, start_ref, out_ref):
    rows = x_ref.shape[1] - 2

    def step(t, state):
        query = filtered_at(x_ref, taps_ref, 0, t)
        gated = filtered_at(x_ref, taps_ref, 1, t) * filtered_at(x_ref, taps_ref, 2, t)
        state = decay_ref[...] * state + gated[None]
        convolved = jnp.sum(resid_ref[...] * state, axis=0)
        out_ref[t] = query * (convolved + skip_ref[...] * gated)
        return state

    lax.fori_loop(0, rows, step, start_ref[...], unroll=8)


def block_kernel(
    peers, digits, x_ref, taps_ref, decay_ref, resid_ref, skip_ref, lift_ref, keep_ref, out_ref,
    end_ref, start_ref, held, slots, send_sem, recv_sem,
):
    me = lax.axis_index("cx") * 2 + lax.axis_index("core")
    tp = lax.axis_index("tp")

    def device(i):
        return (i // 2, i % 2, tp)

    steps = []
    width = 1
    for r, digit in enumerate(digits):
        steps.extend((r, d * width) for d in range(1, digit))
        width *= digit

    barrier = pltpu.get_barrier_semaphore()
    for _, by in steps:
        for peer in ((me + by) % peers, (me + peers - by) % peers):
            pl.semaphore_signal(barrier, inc=1, device_id=device(peer), device_id_type=MESH)
    local_end_kernel(x_ref, taps_ref, decay_ref, end_ref)
    pl.semaphore_wait(barrier, 2 * len(steps))

    held[0] = end_ref[...]
    start_ref[...] = jnp.zeros(start_ref.shape, jnp.float32)
    copies = []
    for r in range(len(digits)):
        mine = [(n, by) for n, (q, by) in enumerate(steps) if q == r]
        for n, by in mine:
            copy = pltpu.make_async_remote_copy(
                src_ref=held.at[r],
                dst_ref=slots.at[n],
                send_sem=send_sem.at[n],
                recv_sem=recv_sem.at[n],
                device_id=device((me + by) % peers),
                device_id_type=MESH,
            )
            copy.start()
            copies.append(copy)
        grown = held[r]
        for n, by in mine:
            copies[n].wait_recv()
            got = jnp.where(me >= by, slots[n], 0.0)
            start_ref[...] += lift_ref[n] * got
            grown = grown + keep_ref[n] * got
        if r + 1 < len(digits):
            held[r + 1] = grown
    mixed_kernel(x_ref, taps_ref, decay_ref, resid_ref, skip_ref, start_ref, out_ref)
    for copy in copies:
        copy.wait_send()


def scan_digits(peers):
    digits = [2] if peers % 2 == 0 else []
    peers //= 2 if digits else 1
    while peers > 1:
        digit = 4 if peers % 4 == 0 else 2
        digits.append(digit)
        peers //= digit
    return digits or [2]


def vmem_specs(n):
    return [pl.BlockSpec(memory_space=pltpu.VMEM)] * n


def shifted(array, axes, by):
    peers = 1
    for axis in axes:
        peers *= lax.axis_size(axis)
    pairs = [(i, i + by) for i in range(peers) if i + by < peers]
    return lax.ppermute(array, axes, pairs)


def swapped(array, axis):
    return lax.ppermute(array, axis, [(0, 1), (1, 0)])


def gathered_tp(tokens):
    peers, here = lax.axis_size("tp"), lax.axis_index("tp")
    blocks = [tokens]
    for by in range(1, peers):
        blocks.append(lax.ppermute(tokens, "tp", [(i, (i + by) % peers) for i in range(peers)]))
    stacked = jnp.stack(blocks, axis=0)
    order = (here - jnp.arange(peers)) % peers
    placed = jnp.take(stacked, jnp.argsort(order), axis=0)
    return jnp.transpose(placed, (1, 0, 2)).reshape(tokens.shape[0], -1)


def per_device(tokens, in_weight, conv_taps, decay_rate, residue, skip):
    ctx = ("cx", "core")
    rows = tokens.shape[0]
    chans = in_weight.shape[2]
    poles = decay_rate.shape[0]
    subl = chans // LANES
    core = lax.axis_index("core")
    piece = lax.all_gather(in_weight, "cx", axis=0, tiled=True)
    whole = gathered_tp(tokens)
    split = whole.reshape(rows, -1, 2, in_weight.shape[0])
    mine = jnp.where(core == 0, split[:, :, 0], split[:, :, 1]).reshape(rows, -1)
    theirs = jnp.where(core == 0, split[:, :, 1], split[:, :, 0]).reshape(rows, -1)
    both = jnp.concatenate([mine, swapped(theirs, "core")], axis=0)
    taps = conv_taps.reshape(3, 3, subl, LANES)
    decay = jnp.exp(-decay_rate).reshape(poles, subl, LANES)
    resid = residue.reshape(poles, subl, LANES)
    direct = skip.reshape(subl, LANES)
    peers = lax.axis_size("cx") * lax.axis_size("core")
    digits = scan_digits(peers)
    strides, width = [], 1
    for digit in digits:
        strides.extend(d * width for d in range(1, digit))
        width *= digit
    copies = len(strides)
    widths = jnp.asarray(strides, jnp.float32)[:, None, None]
    lift = jnp.exp(-decay_rate[None] * (rows * (widths - 1.0))).reshape(copies, poles, subl, LANES)
    keep = jnp.exp(-decay_rate[None] * (rows * widths)).reshape(copies, poles, subl, LANES)
    (taps, decay, resid, direct, lift, keep), both = lax.optimization_barrier(
        ((taps, decay, resid, direct, lift, keep), both)
    )
    theirs_part = jnp.stack(
        [jnp.dot(both[rows:], piece[:, g, :], preferred_element_type=jnp.float32) for g in range(3)],
        axis=0,
    )
    arrived = swapped(theirs_part, "core")
    mine_part = jnp.stack(
        [jnp.dot(both[:rows], piece[:, g, :], preferred_element_type=jnp.float32) for g in range(3)],
        axis=0,
    )
    sums = mine_part + arrived
    projected = sums.astype(jnp.bfloat16)
    edge_out = shifted(projected[:, rows - 2 :, :], ctx, 1)
    extended = jnp.concatenate([edge_out, projected], axis=1).reshape(3, rows + 2, subl, LANES)
    x = lax.optimization_barrier(extended).astype(jnp.float32)
    state_shape = (poles, subl, LANES)
    out = pl.pallas_call(
        functools.partial(block_kernel, peers, digits),
        out_shape=jax.ShapeDtypeStruct((rows, subl, LANES), jnp.float32),
        in_specs=vmem_specs(7),
        out_specs=pl.BlockSpec(memory_space=pltpu.VMEM),
        scratch_shapes=[
            pltpu.VMEM(state_shape, jnp.float32),
            pltpu.VMEM(state_shape, jnp.float32),
            pltpu.VMEM((len(digits),) + state_shape, jnp.float32),
            pltpu.VMEM((copies,) + state_shape, jnp.float32),
            pltpu.SemaphoreType.DMA((copies,)),
            pltpu.SemaphoreType.DMA((copies,)),
        ],
        compiler_params=pltpu.CompilerParams(collective_id=0, has_side_effects=True),
    )(x, taps, decay, resid, direct, lift, keep)
    return out.reshape(rows, chans).astype(jnp.bfloat16)


def solution(mesh):
    ctx, tp = mesh.shape["ctx"], mesh.shape["tp"]
    split = jax.sharding.Mesh(mesh.devices.reshape(ctx // 2, 2, tp), ("cx", "core", "tp"))
    c = ("cx", "core")
    placed = (
        P(c, "tp"),
        P(c, None, "tp"),
        P(None, None, "tp"),
        P(None, "tp"),
        P(None, "tp"),
        P("tp"),
    )
    return jax.shard_map(
        per_device, mesh=split, in_specs=placed, out_specs=P(c, "tp"), check_vma=False
    )
```

```python
import functools

import jax
import jax.numpy as jnp
from jax import lax
from jax.experimental import pallas as pl
from jax.experimental.pallas import tpu as pltpu
from jax.sharding import PartitionSpec as P

MESH = pl.DeviceIdType.MESH

LANES = 128


def filtered_at(x_ref, taps_ref, g, t):
    return (
        taps_ref[0, g] * x_ref[g, t + 2].astype(jnp.float32)
        + taps_ref[1, g] * x_ref[g, t + 1].astype(jnp.float32)
        + taps_ref[2, g] * x_ref[g, t].astype(jnp.float32)
    )


def local_end_kernel(x_ref, taps_ref, decay_ref, end_ref):
    rows = x_ref.shape[1] - 2

    def step(t, state):
        gated = filtered_at(x_ref, taps_ref, 1, t) * filtered_at(x_ref, taps_ref, 2, t)
        return decay_ref[...] * state + gated[None]

    end_ref[...] = lax.fori_loop(
        0, rows, step, jnp.zeros(end_ref.shape, jnp.float32), unroll=8
    )


def mixed_kernel(x_ref, taps_ref, decay_ref, resid_ref, skip_ref, start_ref, out_ref):
    rows = x_ref.shape[1] - 2

    def step(t, state):
        query = filtered_at(x_ref, taps_ref, 0, t)
        gated = filtered_at(x_ref, taps_ref, 1, t) * filtered_at(x_ref, taps_ref, 2, t)
        state = decay_ref[...] * state + gated[None]
        convolved = jnp.sum(resid_ref[...] * state, axis=0)
        out_ref[t] = (query * (convolved + skip_ref[...] * gated)).astype(out_ref.dtype)
        return state

    lax.fori_loop(0, rows, step, start_ref[...], unroll=8)


def block_kernel(
    peers, digits, x_ref, taps_ref, decay_ref, resid_ref, skip_ref, lift_ref, keep_ref, out_ref,
    end_ref, start_ref, held, slots, send_sem, recv_sem,
):
    me = lax.axis_index("cx") * 2 + lax.axis_index("core")
    tp = lax.axis_index("tp")

    def device(i):
        return (i // 2, i % 2, tp)

    steps = []
    width = 1
    for r, digit in enumerate(digits):
        steps.extend((r, d * width) for d in range(1, digit))
        width *= digit

    barrier = pltpu.get_barrier_semaphore()
    for _, by in steps:
        for peer in ((me + by) % peers, (me + peers - by) % peers):
            pl.semaphore_signal(barrier, inc=1, device_id=device(peer), device_id_type=MESH)
    local_end_kernel(x_ref, taps_ref, decay_ref, end_ref)
    pl.semaphore_wait(barrier, 2 * len(steps))

    held[0] = end_ref[...]
    start_ref[...] = jnp.zeros(start_ref.shape, jnp.float32)
    copies = []
    for r in range(len(digits)):
        mine = [(n, by) for n, (q, by) in enumerate(steps) if q == r]
        for n, by in mine:
            copy = pltpu.make_async_remote_copy(
                src_ref=held.at[r],
                dst_ref=slots.at[n],
                send_sem=send_sem.at[n],
                recv_sem=recv_sem.at[n],
                device_id=device((me + by) % peers),
                device_id_type=MESH,
            )
            copy.start()
            copies.append(copy)
        grown = held[r]
        for n, by in mine:
            copies[n].wait_recv()
            got = jnp.where(me >= by, slots[n], 0.0)
            start_ref[...] += lift_ref[n] * got
            grown = grown + keep_ref[n] * got
        if r + 1 < len(digits):
            held[r + 1] = grown
    mixed_kernel(x_ref, taps_ref, decay_ref, resid_ref, skip_ref, start_ref, out_ref)
    for copy in copies:
        copy.wait_send()


def scan_digits(peers):
    digits = [2] if peers % 2 == 0 else []
    peers //= 2 if digits else 1
    while peers > 1:
        digit = 4 if peers % 4 == 0 else 2
        digits.append(digit)
        peers //= digit
    return digits or [2]


def vmem_specs(n):
    return [pl.BlockSpec(memory_space=pltpu.VMEM)] * n


def shifted(array, axes, by):
    peers = 1
    for axis in axes:
        peers *= lax.axis_size(axis)
    pairs = [(i, i + by) for i in range(peers) if i + by < peers]
    return lax.ppermute(array, axes, pairs)


def swapped(array, axis):
    return lax.ppermute(array, axis, [(0, 1), (1, 0)])


def gathered_tp(tokens):
    peers, here = lax.axis_size("tp"), lax.axis_index("tp")
    blocks = [tokens]
    for by in range(1, peers):
        blocks.append(lax.ppermute(tokens, "tp", [(i, (i + by) % peers) for i in range(peers)]))
    stacked = jnp.stack(blocks, axis=0)
    order = (here - jnp.arange(peers)) % peers
    placed = jnp.take(stacked, jnp.argsort(order), axis=0)
    return jnp.transpose(placed, (1, 0, 2)).reshape(tokens.shape[0], -1)


def per_device(tokens, in_weight, conv_taps, decay_rate, residue, skip):
    ctx = ("cx", "core")
    rows = tokens.shape[0]
    chans = in_weight.shape[2]
    poles = decay_rate.shape[0]
    subl = chans // LANES
    core = lax.axis_index("core")
    piece = lax.all_gather(in_weight, "cx", axis=0, tiled=True)
    whole = gathered_tp(tokens)
    split = whole.reshape(rows, -1, 2, in_weight.shape[0])
    mine = jnp.where(core == 0, split[:, :, 0], split[:, :, 1]).reshape(rows, -1)
    theirs = jnp.where(core == 0, split[:, :, 1], split[:, :, 0]).reshape(rows, -1)
    both = jnp.concatenate([mine, swapped(theirs, "core")], axis=0)
    taps = conv_taps.reshape(3, 3, subl, LANES)
    decay = jnp.exp(-decay_rate).reshape(poles, subl, LANES)
    resid = residue.reshape(poles, subl, LANES)
    direct = skip.reshape(subl, LANES)
    peers = lax.axis_size("cx") * lax.axis_size("core")
    digits = scan_digits(peers)
    strides, width = [], 1
    for digit in digits:
        strides.extend(d * width for d in range(1, digit))
        width *= digit
    copies = len(strides)
    widths = jnp.asarray(strides, jnp.float32)[:, None, None]
    lift = jnp.exp(-decay_rate[None] * (rows * (widths - 1.0))).reshape(copies, poles, subl, LANES)
    keep = jnp.exp(-decay_rate[None] * (rows * widths)).reshape(copies, poles, subl, LANES)
    (taps, decay, resid, direct, lift, keep), both = lax.optimization_barrier(
        ((taps, decay, resid, direct, lift, keep), both)
    )
    theirs_part = jnp.stack(
        [jnp.dot(both[rows:], piece[:, g, :], preferred_element_type=jnp.float32) for g in range(3)],
        axis=0,
    )
    arrived = swapped(theirs_part, "core")
    mine_part = jnp.stack(
        [jnp.dot(both[:rows], piece[:, g, :], preferred_element_type=jnp.float32) for g in range(3)],
        axis=0,
    )
    sums = mine_part + arrived
    projected = sums.astype(jnp.bfloat16)
    edge_out = shifted(projected[:, rows - 2 :, :], ctx, 1)
    extended = jnp.concatenate([edge_out, projected], axis=1).reshape(3, rows + 2, subl, LANES)
    x = lax.optimization_barrier(extended)
    state_shape = (poles, subl, LANES)
    out = pl.pallas_call(
        functools.partial(block_kernel, peers, digits),
        out_shape=jax.ShapeDtypeStruct((rows, subl, LANES), jnp.bfloat16),
        in_specs=vmem_specs(7),
        out_specs=pl.BlockSpec(memory_space=pltpu.VMEM),
        scratch_shapes=[
            pltpu.VMEM(state_shape, jnp.float32),
            pltpu.VMEM(state_shape, jnp.float32),
            pltpu.VMEM((len(digits),) + state_shape, jnp.float32),
            pltpu.VMEM((copies,) + state_shape, jnp.float32),
            pltpu.SemaphoreType.DMA((copies,)),
            pltpu.SemaphoreType.DMA((copies,)),
        ],
        compiler_params=pltpu.CompilerParams(collective_id=0, has_side_effects=True),
    )(x, taps, decay, resid, direct, lift, keep)
    return out.reshape(rows, chans)


def solution(mesh):
    ctx, tp = mesh.shape["ctx"], mesh.shape["tp"]
    split = jax.sharding.Mesh(mesh.devices.reshape(ctx // 2, 2, tp), ("cx", "core", "tp"))
    c = ("cx", "core")
    placed = (
        P(c, "tp"),
        P(c, None, "tp"),
        P(None, None, "tp"),
        P(None, "tp"),
        P(None, "tp"),
        P("tp"),
    )
    return jax.shard_map(
        per_device, mesh=split, in_specs=placed, out_specs=P(c, "tp"), check_vma=False
    )
```

```python
import functools

import jax
import jax.numpy as jnp
from jax import lax
from jax.experimental import pallas as pl
from jax.experimental.pallas import tpu as pltpu
from jax.sharding import PartitionSpec as P

MESH = pl.DeviceIdType.MESH

LANES = 128


def filtered_at(x_ref, taps_ref, g, t):
    return (
        taps_ref[0, g] * x_ref[g, t + 2].astype(jnp.float32)
        + taps_ref[1, g] * x_ref[g, t + 1].astype(jnp.float32)
        + taps_ref[2, g] * x_ref[g, t].astype(jnp.float32)
    )


def local_end_kernel(x_ref, taps_ref, decay_ref, end_ref):
    rows = x_ref.shape[1] - 2

    def step(t, state):
        gated = filtered_at(x_ref, taps_ref, 1, t) * filtered_at(x_ref, taps_ref, 2, t)
        return decay_ref[...] * state + gated[None]

    end_ref[...] = lax.fori_loop(
        0, rows, step, jnp.zeros(end_ref.shape, jnp.float32), unroll=8
    )


def mixed_kernel(x_ref, taps_ref, decay_ref, resid_ref, skip_ref, start_ref, out_ref):
    rows = x_ref.shape[1] - 2
    run = 16
    subl = x_ref.shape[2]

    def block(b, state):
        values = []
        for i in range(run):
            t = b * run + i
            query = filtered_at(x_ref, taps_ref, 0, t)
            gated = filtered_at(x_ref, taps_ref, 1, t) * filtered_at(x_ref, taps_ref, 2, t)
            state = decay_ref[...] * state + gated[None]
            convolved = jnp.sum(resid_ref[...] * state, axis=0)
            values.append(query * (convolved + skip_ref[...] * gated))
        tiles = jnp.swapaxes(jnp.stack(values, axis=0), 0, 1)
        first = pl.multiple_of(b * run, run)
        for s in range(subl):
            out_ref[pl.ds(first, run), pl.ds(s * LANES, LANES)] = tiles[s].astype(out_ref.dtype)
        return state

    lax.fori_loop(0, rows // run, block, start_ref[...])


def block_kernel(
    peers, digits, x_ref, taps_ref, decay_ref, resid_ref, skip_ref, lift_ref, keep_ref, out_ref,
    end_ref, start_ref, held, slots, send_sem, recv_sem,
):
    me = lax.axis_index("cx") * 2 + lax.axis_index("core")
    tp = lax.axis_index("tp")

    def device(i):
        return (i // 2, i % 2, tp)

    steps = []
    width = 1
    for r, digit in enumerate(digits):
        steps.extend((r, d * width) for d in range(1, digit))
        width *= digit

    barrier = pltpu.get_barrier_semaphore()
    for _, by in steps:
        for peer in ((me + by) % peers, (me + peers - by) % peers):
            pl.semaphore_signal(barrier, inc=1, device_id=device(peer), device_id_type=MESH)
    local_end_kernel(x_ref, taps_ref, decay_ref, end_ref)
    pl.semaphore_wait(barrier, 2 * len(steps))

    held[0] = end_ref[...]
    start_ref[...] = jnp.zeros(start_ref.shape, jnp.float32)
    copies = []
    for r in range(len(digits)):
        mine = [(n, by) for n, (q, by) in enumerate(steps) if q == r]
        for n, by in mine:
            copy = pltpu.make_async_remote_copy(
                src_ref=held.at[r],
                dst_ref=slots.at[n],
                send_sem=send_sem.at[n],
                recv_sem=recv_sem.at[n],
                device_id=device((me + by) % peers),
                device_id_type=MESH,
            )
            copy.start()
            copies.append(copy)
        grown = held[r]
        for n, by in mine:
            copies[n].wait_recv()
            got = jnp.where(me >= by, slots[n], 0.0)
            start_ref[...] += lift_ref[n] * got
            grown = grown + keep_ref[n] * got
        if r + 1 < len(digits):
            held[r + 1] = grown
    mixed_kernel(x_ref, taps_ref, decay_ref, resid_ref, skip_ref, start_ref, out_ref)
    for copy in copies:
        copy.wait_send()


def scan_digits(peers):
    digits = [2] if peers % 2 == 0 else []
    peers //= 2 if digits else 1
    while peers > 1:
        digit = 4 if peers % 4 == 0 else 2
        digits.append(digit)
        peers //= digit
    return digits or [2]


def vmem_specs(n):
    return [pl.BlockSpec(memory_space=pltpu.VMEM)] * n


def shifted(array, axes, by):
    peers = 1
    for axis in axes:
        peers *= lax.axis_size(axis)
    pairs = [(i, i + by) for i in range(peers) if i + by < peers]
    return lax.ppermute(array, axes, pairs)


def swapped(array, axis):
    return lax.ppermute(array, axis, [(0, 1), (1, 0)])


def gathered_tp(tokens):
    peers, here = lax.axis_size("tp"), lax.axis_index("tp")
    blocks = [tokens]
    for by in range(1, peers):
        blocks.append(lax.ppermute(tokens, "tp", [(i, (i + by) % peers) for i in range(peers)]))
    stacked = jnp.stack(blocks, axis=0)
    order = (here - jnp.arange(peers)) % peers
    placed = jnp.take(stacked, jnp.argsort(order), axis=0)
    return jnp.transpose(placed, (1, 0, 2)).reshape(tokens.shape[0], -1)


def per_device(tokens, in_weight, conv_taps, decay_rate, residue, skip):
    ctx = ("cx", "core")
    rows = tokens.shape[0]
    chans = in_weight.shape[2]
    poles = decay_rate.shape[0]
    subl = chans // LANES
    core = lax.axis_index("core")
    piece = lax.all_gather(in_weight, "cx", axis=0, tiled=True)
    whole = gathered_tp(tokens)
    split = whole.reshape(rows, -1, 2, in_weight.shape[0])
    mine = jnp.where(core == 0, split[:, :, 0], split[:, :, 1]).reshape(rows, -1)
    theirs = jnp.where(core == 0, split[:, :, 1], split[:, :, 0]).reshape(rows, -1)
    both = jnp.concatenate([mine, swapped(theirs, "core")], axis=0)
    taps = conv_taps.reshape(3, 3, subl, LANES)
    decay = jnp.exp(-decay_rate).reshape(poles, subl, LANES)
    resid = residue.reshape(poles, subl, LANES)
    direct = skip.reshape(subl, LANES)
    peers = lax.axis_size("cx") * lax.axis_size("core")
    digits = scan_digits(peers)
    strides, width = [], 1
    for digit in digits:
        strides.extend(d * width for d in range(1, digit))
        width *= digit
    copies = len(strides)
    widths = jnp.asarray(strides, jnp.float32)[:, None, None]
    lift = jnp.exp(-decay_rate[None] * (rows * (widths - 1.0))).reshape(copies, poles, subl, LANES)
    keep = jnp.exp(-decay_rate[None] * (rows * widths)).reshape(copies, poles, subl, LANES)
    (taps, decay, resid, direct, lift, keep), both = lax.optimization_barrier(
        ((taps, decay, resid, direct, lift, keep), both)
    )
    theirs_part = jnp.stack(
        [jnp.dot(both[rows:], piece[:, g, :], preferred_element_type=jnp.float32) for g in range(3)],
        axis=0,
    )
    arrived = swapped(theirs_part, "core")
    mine_part = jnp.stack(
        [jnp.dot(both[:rows], piece[:, g, :], preferred_element_type=jnp.float32) for g in range(3)],
        axis=0,
    )
    sums = mine_part + arrived
    projected = sums.astype(jnp.bfloat16)
    edge_out = shifted(projected[:, rows - 2 :, :], ctx, 1)
    extended = jnp.concatenate([edge_out, projected], axis=1).reshape(3, rows + 2, subl, LANES)
    x = lax.optimization_barrier(extended)
    state_shape = (poles, subl, LANES)
    out = pl.pallas_call(
        functools.partial(block_kernel, peers, digits),
        out_shape=jax.ShapeDtypeStruct((rows, chans), jnp.bfloat16),
        in_specs=vmem_specs(7),
        out_specs=pl.BlockSpec(memory_space=pltpu.VMEM),
        scratch_shapes=[
            pltpu.VMEM(state_shape, jnp.float32),
            pltpu.VMEM(state_shape, jnp.float32),
            pltpu.VMEM((len(digits),) + state_shape, jnp.float32),
            pltpu.VMEM((copies,) + state_shape, jnp.float32),
            pltpu.SemaphoreType.DMA((copies,)),
            pltpu.SemaphoreType.DMA((copies,)),
        ],
        compiler_params=pltpu.CompilerParams(collective_id=0, has_side_effects=True),
    )(x, taps, decay, resid, direct, lift, keep)
    return out


def solution(mesh):
    ctx, tp = mesh.shape["ctx"], mesh.shape["tp"]
    split = jax.sharding.Mesh(mesh.devices.reshape(ctx // 2, 2, tp), ("cx", "core", "tp"))
    c = ("cx", "core")
    placed = (
        P(c, "tp"),
        P(c, None, "tp"),
        P(None, None, "tp"),
        P(None, "tp"),
        P(None, "tp"),
        P("tp"),
    )
    return jax.shard_map(
        per_device, mesh=split, in_specs=placed, out_specs=P(c, "tp"), check_vma=False
    )
```

```python
import functools

import jax
import jax.numpy as jnp
from jax import lax
from jax.experimental import pallas as pl
from jax.experimental.pallas import tpu as pltpu
from jax.sharding import PartitionSpec as P

MESH = pl.DeviceIdType.MESH

LANES = 128


def filtered_at(x_ref, taps_ref, g, t):
    return (
        taps_ref[0, g] * x_ref[g, t + 2]
        + taps_ref[1, g] * x_ref[g, t + 1]
        + taps_ref[2, g] * x_ref[g, t]
    )


def local_end_kernel(x_ref, taps_ref, decay_ref, end_ref):
    rows = x_ref.shape[1] - 2

    def step(t, state):
        gated = filtered_at(x_ref, taps_ref, 1, t) * filtered_at(x_ref, taps_ref, 2, t)
        return decay_ref[...] * state + gated[None]

    end_ref[...] = lax.fori_loop(
        0, rows, step, jnp.zeros(end_ref.shape, jnp.float32), unroll=8
    )


def mixed_kernel(x_ref, taps_ref, decay_ref, resid_ref, skip_ref, start_ref, out_ref):
    rows = x_ref.shape[1] - 2
    run = 16
    subl = x_ref.shape[2]

    def block(b, state):
        values = []
        for i in range(run):
            t = b * run + i
            query = filtered_at(x_ref, taps_ref, 0, t)
            gated = filtered_at(x_ref, taps_ref, 1, t) * filtered_at(x_ref, taps_ref, 2, t)
            state = decay_ref[...] * state + gated[None]
            convolved = jnp.sum(resid_ref[...] * state, axis=0)
            values.append(query * (convolved + skip_ref[...] * gated))
        tiles = jnp.swapaxes(jnp.stack(values, axis=0), 0, 1)
        first = pl.multiple_of(b * run, run)
        for s in range(subl):
            out_ref[pl.ds(first, run), pl.ds(s * LANES, LANES)] = tiles[s].astype(out_ref.dtype)
        return state

    lax.fori_loop(0, rows // run, block, start_ref[...])


def to_positions(proj_ref, edge_ref, x_ref):
    run = 16
    subl = x_ref.shape[2]
    x_ref[:, 0:2] = edge_ref[...].astype(jnp.float32)
    for g in range(proj_ref.shape[0]):
        for b in range(proj_ref.shape[1] // run):
            rows_ = proj_ref[g, b * run : (b + 1) * run, :].astype(jnp.float32)
            cols = jnp.stack([rows_[:, s * LANES : (s + 1) * LANES] for s in range(subl)], axis=0)
            x_ref[g, 2 + b * run : 2 + (b + 1) * run] = jnp.swapaxes(cols, 0, 1)


def block_kernel(
    peers, digits, proj_ref, edge_ref, taps_ref, decay_ref, resid_ref, skip_ref, lift_ref, keep_ref,
    out_ref, x_ref, end_ref, start_ref, held, slots, send_sem, recv_sem,
):
    me = lax.axis_index("cx") * 2 + lax.axis_index("core")
    tp = lax.axis_index("tp")

    def device(i):
        return (i // 2, i % 2, tp)

    steps = []
    width = 1
    for r, digit in enumerate(digits):
        steps.extend((r, d * width) for d in range(1, digit))
        width *= digit

    barrier = pltpu.get_barrier_semaphore()
    for _, by in steps:
        for peer in ((me + by) % peers, (me + peers - by) % peers):
            pl.semaphore_signal(barrier, inc=1, device_id=device(peer), device_id_type=MESH)
    to_positions(proj_ref, edge_ref, x_ref)
    local_end_kernel(x_ref, taps_ref, decay_ref, end_ref)
    pl.semaphore_wait(barrier, 2 * len(steps))

    held[0] = end_ref[...]
    start_ref[...] = jnp.zeros(start_ref.shape, jnp.float32)
    copies = []
    for r in range(len(digits)):
        mine = [(n, by) for n, (q, by) in enumerate(steps) if q == r]
        for n, by in mine:
            copy = pltpu.make_async_remote_copy(
                src_ref=held.at[r],
                dst_ref=slots.at[n],
                send_sem=send_sem.at[n],
                recv_sem=recv_sem.at[n],
                device_id=device((me + by) % peers),
                device_id_type=MESH,
            )
            copy.start()
            copies.append(copy)
        grown = held[r]
        for n, by in mine:
            copies[n].wait_recv()
            got = jnp.where(me >= by, slots[n], 0.0)
            start_ref[...] += lift_ref[n] * got
            grown = grown + keep_ref[n] * got
        if r + 1 < len(digits):
            held[r + 1] = grown
    mixed_kernel(x_ref, taps_ref, decay_ref, resid_ref, skip_ref, start_ref, out_ref)
    for copy in copies:
        copy.wait_send()


def scan_digits(peers):
    digits = [2] if peers % 2 == 0 else []
    peers //= 2 if digits else 1
    while peers > 1:
        digit = 4 if peers % 4 == 0 else 2
        digits.append(digit)
        peers //= digit
    return digits or [2]


def vmem_specs(n):
    return [pl.BlockSpec(memory_space=pltpu.VMEM)] * n


def shifted(array, axes, by):
    peers = 1
    for axis in axes:
        peers *= lax.axis_size(axis)
    pairs = [(i, i + by) for i in range(peers) if i + by < peers]
    return lax.ppermute(array, axes, pairs)


def swapped(array, axis):
    return lax.ppermute(array, axis, [(0, 1), (1, 0)])


def gathered_tp(tokens):
    peers, here = lax.axis_size("tp"), lax.axis_index("tp")
    blocks = [tokens]
    for by in range(1, peers):
        blocks.append(lax.ppermute(tokens, "tp", [(i, (i + by) % peers) for i in range(peers)]))
    stacked = jnp.stack(blocks, axis=0)
    order = (here - jnp.arange(peers)) % peers
    placed = jnp.take(stacked, jnp.argsort(order), axis=0)
    return jnp.transpose(placed, (1, 0, 2)).reshape(tokens.shape[0], -1)


def per_device(tokens, in_weight, conv_taps, decay_rate, residue, skip):
    ctx = ("cx", "core")
    rows = tokens.shape[0]
    chans = in_weight.shape[2]
    poles = decay_rate.shape[0]
    subl = chans // LANES
    core = lax.axis_index("core")
    piece = lax.all_gather(in_weight, "cx", axis=0, tiled=True)
    whole = gathered_tp(tokens)
    split = whole.reshape(rows, -1, 2, in_weight.shape[0])
    mine = jnp.where(core == 0, split[:, :, 0], split[:, :, 1]).reshape(rows, -1)
    theirs = jnp.where(core == 0, split[:, :, 1], split[:, :, 0]).reshape(rows, -1)
    both = jnp.concatenate([mine, swapped(theirs, "core")], axis=0)
    taps = conv_taps.reshape(3, 3, subl, LANES)
    decay = jnp.exp(-decay_rate).reshape(poles, subl, LANES)
    resid = residue.reshape(poles, subl, LANES)
    direct = skip.reshape(subl, LANES)
    peers = lax.axis_size("cx") * lax.axis_size("core")
    digits = scan_digits(peers)
    strides, width = [], 1
    for digit in digits:
        strides.extend(d * width for d in range(1, digit))
        width *= digit
    copies = len(strides)
    widths = jnp.asarray(strides, jnp.float32)[:, None, None]
    lift = jnp.exp(-decay_rate[None] * (rows * (widths - 1.0))).reshape(copies, poles, subl, LANES)
    keep = jnp.exp(-decay_rate[None] * (rows * widths)).reshape(copies, poles, subl, LANES)
    (taps, decay, resid, direct, lift, keep), both = lax.optimization_barrier(
        ((taps, decay, resid, direct, lift, keep), both)
    )
    theirs_part = jnp.stack(
        [jnp.dot(both[rows:], piece[:, g, :], preferred_element_type=jnp.float32) for g in range(3)],
        axis=0,
    )
    arrived = swapped(theirs_part, "core")
    mine_part = jnp.stack(
        [jnp.dot(both[:rows], piece[:, g, :], preferred_element_type=jnp.float32) for g in range(3)],
        axis=0,
    )
    sums = mine_part + arrived
    projected = sums.astype(jnp.bfloat16)
    edge_out = shifted(projected[:, rows - 2 :, :], ctx, 1)
    edge = edge_out.reshape(3, 2, subl, LANES)
    projected, edge = lax.optimization_barrier((projected, edge))
    state_shape = (poles, subl, LANES)
    out = pl.pallas_call(
        functools.partial(block_kernel, peers, digits),
        out_shape=jax.ShapeDtypeStruct((rows, chans), jnp.bfloat16),
        in_specs=vmem_specs(8),
        out_specs=pl.BlockSpec(memory_space=pltpu.VMEM),
        scratch_shapes=[
            pltpu.VMEM((3, rows + 2, subl, LANES), jnp.float32),
            pltpu.VMEM(state_shape, jnp.float32),
            pltpu.VMEM(state_shape, jnp.float32),
            pltpu.VMEM((len(digits),) + state_shape, jnp.float32),
            pltpu.VMEM((copies,) + state_shape, jnp.float32),
            pltpu.SemaphoreType.DMA((copies,)),
            pltpu.SemaphoreType.DMA((copies,)),
        ],
        compiler_params=pltpu.CompilerParams(collective_id=0, has_side_effects=True),
    )(projected, edge, taps, decay, resid, direct, lift, keep)
    return out


def solution(mesh):
    ctx, tp = mesh.shape["ctx"], mesh.shape["tp"]
    split = jax.sharding.Mesh(mesh.devices.reshape(ctx // 2, 2, tp), ("cx", "core", "tp"))
    c = ("cx", "core")
    placed = (
        P(c, "tp"),
        P(c, None, "tp"),
        P(None, None, "tp"),
        P(None, "tp"),
        P(None, "tp"),
        P("tp"),
    )
    return jax.shard_map(
        per_device, mesh=split, in_specs=placed, out_specs=P(c, "tp"), check_vma=False
    )
```

```python
import functools

import jax
import jax.numpy as jnp
from jax import lax
from jax.experimental import pallas as pl
from jax.experimental.pallas import tpu as pltpu
from jax.sharding import PartitionSpec as P

MESH = pl.DeviceIdType.MESH

LANES = 128


def filtered_at(x_ref, taps_ref, g, t):
    return (
        taps_ref[0, g] * x_ref[g, t + 2]
        + taps_ref[1, g] * x_ref[g, t + 1]
        + taps_ref[2, g] * x_ref[g, t]
    )


def local_end_kernel(x_ref, taps_ref, decay_ref, end_ref):
    rows = x_ref.shape[1] - 2

    def step(t, state):
        gated = filtered_at(x_ref, taps_ref, 1, t) * filtered_at(x_ref, taps_ref, 2, t)
        return decay_ref[...] * state + gated[None]

    end_ref[...] = lax.fori_loop(
        0, rows, step, jnp.zeros(end_ref.shape, jnp.float32), unroll=8
    )


def mixed_kernel(x_ref, taps_ref, decay_ref, resid_ref, skip_ref, start_ref, out_ref):
    rows = x_ref.shape[1] - 2
    run = 16
    subl = x_ref.shape[2]

    def block(b, state):
        values = []
        for i in range(run):
            t = b * run + i
            query = filtered_at(x_ref, taps_ref, 0, t)
            gated = filtered_at(x_ref, taps_ref, 1, t) * filtered_at(x_ref, taps_ref, 2, t)
            state = decay_ref[...] * state + gated[None]
            convolved = jnp.sum(resid_ref[...] * state, axis=0)
            values.append(query * (convolved + skip_ref[...] * gated))
        tiles = jnp.swapaxes(jnp.stack(values, axis=0), 0, 1)
        first = pl.multiple_of(b * run, run)
        for s in range(subl):
            out_ref[pl.ds(first, run), pl.ds(s * LANES, LANES)] = tiles[s].astype(out_ref.dtype)
        return state

    lax.fori_loop(0, rows // run, block, start_ref[...])


def to_positions(proj_ref, edge_ref, x_ref):
    run = 16
    subl = x_ref.shape[2]
    x_ref[:, 0:2] = edge_ref[...].astype(jnp.float32)
    for g in range(proj_ref.shape[0]):
        for b in range(proj_ref.shape[1] // run):
            rows_ = proj_ref[g, b * run : (b + 1) * run, :].astype(jnp.float32)
            cols = jnp.stack([rows_[:, s * LANES : (s + 1) * LANES] for s in range(subl)], axis=0)
            x_ref[g, 2 + b * run : 2 + (b + 1) * run] = jnp.swapaxes(cols, 0, 1)


def block_kernel(
    peers, digits, proj_ref, edge_ref, taps_ref, decay_ref, resid_ref, skip_ref, lift_ref, keep_ref,
    out_ref, x_ref, end_ref, start_ref, held, slots, send_sem, recv_sem,
):
    me = lax.axis_index("cx") * 2 + lax.axis_index("core")
    tp = lax.axis_index("tp")

    def device(i):
        return (i // 2, i % 2, tp)

    steps = []
    width = 1
    for r, digit in enumerate(digits):
        steps.extend((r, d * width) for d in range(1, digit))
        width *= digit

    barrier = pltpu.get_barrier_semaphore()
    for _, by in steps:
        for peer in ((me + by) % peers, (me + peers - by) % peers):
            pl.semaphore_signal(barrier, inc=1, device_id=device(peer), device_id_type=MESH)
    to_positions(proj_ref, edge_ref, x_ref)
    local_end_kernel(x_ref, taps_ref, decay_ref, end_ref)
    pl.semaphore_wait(barrier, 2 * len(steps))

    held[0] = end_ref[...]
    start_ref[...] = jnp.zeros(start_ref.shape, jnp.float32)
    copies = []
    for r in range(len(digits)):
        mine = [(n, by) for n, (q, by) in enumerate(steps) if q == r]
        if r + 1 < len(digits):
            held[r + 1] = held[r]
        for n, by in mine:
            copy = pltpu.make_async_remote_copy(
                src_ref=held.at[r],
                dst_ref=slots.at[n],
                send_sem=send_sem.at[n],
                recv_sem=recv_sem.at[n],
                device_id=device(jnp.minimum(me + by, peers - 1)),
                device_id_type=MESH,
            )

            @pl.when(me + by < peers)
            def _():
                copy.start()

            copies.append((copy, by))
        for n, by in mine:
            copy = copies[n][0]

            @pl.when(me >= by)
            def _():
                copy.wait_recv()
                got = slots[n]
                start_ref[...] += lift_ref[n] * got
                if r + 1 < len(digits):
                    held[r + 1] = held[r + 1] + keep_ref[n] * got

    mixed_kernel(x_ref, taps_ref, decay_ref, resid_ref, skip_ref, start_ref, out_ref)
    for copy, by in copies:

        @pl.when(me + by < peers)
        def _():
            copy.wait_send()


def scan_digits(peers):
    digits = [2] if peers % 2 == 0 else []
    peers //= 2 if digits else 1
    while peers > 1:
        digit = 4 if peers % 4 == 0 else 2
        digits.append(digit)
        peers //= digit
    return digits or [2]


def vmem_specs(n):
    return [pl.BlockSpec(memory_space=pltpu.VMEM)] * n


def shifted(array, axes, by):
    peers = 1
    for axis in axes:
        peers *= lax.axis_size(axis)
    pairs = [(i, i + by) for i in range(peers) if i + by < peers]
    return lax.ppermute(array, axes, pairs)


def swapped(array, axis):
    return lax.ppermute(array, axis, [(0, 1), (1, 0)])


def gathered_tp(tokens):
    peers, here = lax.axis_size("tp"), lax.axis_index("tp")
    blocks = [tokens]
    for by in range(1, peers):
        blocks.append(lax.ppermute(tokens, "tp", [(i, (i + by) % peers) for i in range(peers)]))
    stacked = jnp.stack(blocks, axis=0)
    order = (here - jnp.arange(peers)) % peers
    placed = jnp.take(stacked, jnp.argsort(order), axis=0)
    return jnp.transpose(placed, (1, 0, 2)).reshape(tokens.shape[0], -1)


def per_device(tokens, in_weight, conv_taps, decay_rate, residue, skip):
    ctx = ("cx", "core")
    rows = tokens.shape[0]
    chans = in_weight.shape[2]
    poles = decay_rate.shape[0]
    subl = chans // LANES
    core = lax.axis_index("core")
    piece = lax.all_gather(in_weight, "cx", axis=0, tiled=True)
    whole = gathered_tp(tokens)
    split = whole.reshape(rows, -1, 2, in_weight.shape[0])
    mine = jnp.where(core == 0, split[:, :, 0], split[:, :, 1]).reshape(rows, -1)
    theirs = jnp.where(core == 0, split[:, :, 1], split[:, :, 0]).reshape(rows, -1)
    both = jnp.concatenate([mine, swapped(theirs, "core")], axis=0)
    taps = conv_taps.reshape(3, 3, subl, LANES)
    decay = jnp.exp(-decay_rate).reshape(poles, subl, LANES)
    resid = residue.reshape(poles, subl, LANES)
    direct = skip.reshape(subl, LANES)
    peers = lax.axis_size("cx") * lax.axis_size("core")
    digits = scan_digits(peers)
    strides, width = [], 1
    for digit in digits:
        strides.extend(d * width for d in range(1, digit))
        width *= digit
    copies = len(strides)
    widths = jnp.asarray(strides, jnp.float32)[:, None, None]
    lift = jnp.exp(-decay_rate[None] * (rows * (widths - 1.0))).reshape(copies, poles, subl, LANES)
    keep = jnp.exp(-decay_rate[None] * (rows * widths)).reshape(copies, poles, subl, LANES)
    (taps, decay, resid, direct, lift, keep), both = lax.optimization_barrier(
        ((taps, decay, resid, direct, lift, keep), both)
    )
    theirs_part = jnp.stack(
        [jnp.dot(both[rows:], piece[:, g, :], preferred_element_type=jnp.float32) for g in range(3)],
        axis=0,
    )
    arrived = swapped(theirs_part, "core")
    mine_part = jnp.stack(
        [jnp.dot(both[:rows], piece[:, g, :], preferred_element_type=jnp.float32) for g in range(3)],
        axis=0,
    )
    sums = mine_part + arrived
    projected = sums.astype(jnp.bfloat16)
    edge_out = shifted(projected[:, rows - 2 :, :], ctx, 1)
    edge = edge_out.reshape(3, 2, subl, LANES)
    projected, edge = lax.optimization_barrier((projected, edge))
    state_shape = (poles, subl, LANES)
    out = pl.pallas_call(
        functools.partial(block_kernel, peers, digits),
        out_shape=jax.ShapeDtypeStruct((rows, chans), jnp.bfloat16),
        in_specs=vmem_specs(8),
        out_specs=pl.BlockSpec(memory_space=pltpu.VMEM),
        scratch_shapes=[
            pltpu.VMEM((3, rows + 2, subl, LANES), jnp.float32),
            pltpu.VMEM(state_shape, jnp.float32),
            pltpu.VMEM(state_shape, jnp.float32),
            pltpu.VMEM((len(digits),) + state_shape, jnp.float32),
            pltpu.VMEM((copies,) + state_shape, jnp.float32),
            pltpu.SemaphoreType.DMA((copies,)),
            pltpu.SemaphoreType.DMA((copies,)),
        ],
        compiler_params=pltpu.CompilerParams(collective_id=0, has_side_effects=True),
    )(projected, edge, taps, decay, resid, direct, lift, keep)
    return out


def solution(mesh):
    ctx, tp = mesh.shape["ctx"], mesh.shape["tp"]
    split = jax.sharding.Mesh(mesh.devices.reshape(ctx // 2, 2, tp), ("cx", "core", "tp"))
    c = ("cx", "core")
    placed = (
        P(c, "tp"),
        P(c, None, "tp"),
        P(None, None, "tp"),
        P(None, "tp"),
        P(None, "tp"),
        P("tp"),
    )
    return jax.shard_map(
        per_device, mesh=split, in_specs=placed, out_specs=P(c, "tp"), check_vma=False
    )
```
